32 devices in a mesh: section: 2 (over y), seq: 4 (over z), dp: 4 (over x, core).
Axes of the slice: x: 2, y: 2, z: 4, core: 2. Of those that a mesh axis runs over, the one named last changes fastest.
Arguments:
- ends_in: bfloat16 [2, 8, 256, 1024], P('section', 'dp', 'seq'), may hold values from -40 to 40
- segments: int32 [8, 256], P('dp', 'seq'), may hold values from 0 to 7, never falling along the last dimension, each value on 1 to 64 neighbouring positions
- qkv_weight: bfloat16 [2, 1024, 3072], P('section', 'dp'), may hold values from -2 to 2
- out_weight: bfloat16 [2, 1024, 1024], P('section', 'dp'), may hold values from -1 to 1
- up_weight: bfloat16 [2, 1024, 4096], P('section', 'dp'), may hold values from -0.1875 to 0.1875
- down_weight: bfloat16 [2, 4096, 1024], P('section', 'dp'), may hold values from -0.09375 to 0.09375
- gains: bfloat16 [2, 2, 1024], P('section', None, 'dp'), may hold values from 0.5 to 1.5
- shifts: bfloat16 [2, 6, 1024], P('section', None, 'dp'), may hold values from -3 to 3
- up_bias: bfloat16 [2, 4096], P('section', 'dp'), may hold values from -3 to 3
Outputs:
- ends_out: float32 [2, 8, 256, 1024], P('section', 'dp', 'seq')
- qkv_grad: float32 [2, 1024, 3072], P('section', 'dp')
- out_grad: float32 [2, 1024, 1024], P('section', 'dp')
- up_grad: float32 [2, 1024, 4096], P('section', 'dp')
- down_grad: float32 [2, 4096, 1024], P('section', 'dp')
- gains_grad: float32 [2, 2, 1024], P('section', None, 'dp')
- shifts_grad: float32 [2, 6, 1024], P('section', None, 'dp')
- up_bias_grad: float32 [2, 4096], P('section', 'dp')
The draws below stay inside these ranges and needn't reach their ends.
Inputs may be any that keep to these rules, and one draw needn't show every extreme that they name: `segments`: segment numbers never fall along a sequence; every segment is 1 to 64 tokens long, one of them exactly that long.
All inputs are finite; a program needn't handle non-finite values.
Results may differ from the reference program's by a relative error of at most 0.019.
Values may be sent and summed in bfloat16 or wider, within the bound.
A program may use at most 256 MiB of HBM per device.

```python
import math
import jax
import jax.numpy as jnp
import numpy as np
from jax import lax

D = 1024
H = 16
DH = 64
FF = 4096
LEN = 256
NSEQ = 8


def draw_ends_in(key, part):
    noise_key, row_key = jax.random.split(key, 2)
    values = jax.random.normal(noise_key, (2, NSEQ, LEN, D), jnp.float32)
    row_scale = jnp.exp(jax.random.uniform(row_key, (2, NSEQ, LEN, 1), jnp.float32, math.log(0.5), math.log(2.0)))
    values = values * row_scale
    return jnp.clip(values, -40.0, 40.0).astype(jnp.bfloat16)


def draw_qkv_weight(key, part):
    base_key = jax.random.fold_in(key, 0)
    scale_factor = D ** (-0.5)
    base = jax.random.normal(base_key, (2, D, 3 * D), jnp.float32) * scale_factor
    return jnp.clip(base, -2.0, 2.0).astype(jnp.bfloat16)


def level_of(key, shape, cuts, smallest, top_value):
    def one(dim, shards_of):
        draws = jax.random.uniform(jax.random.fold_in(jax.random.fold_in(key, 6), dim), (shards_of,), jnp.float32, smallest / len(cuts), top_value / len(cuts))
        return jnp.repeat(jnp.exp(draws), shape[dim] // shards_of).reshape((-1,) + (1,) * (len(shape) - dim - 1))

    gain = one(*cuts[0])
    for cut in cuts[1:]:
        gain = gain * one(*cut)
    return gain


def profile(count, total, bound, lean):
    portions = [(1 << 20) // math.isqrt(standing ** lean) + 1 for standing in range(2, count + 1)]
    surplus, counts = total - bound - (count - 1), [1] * (count - 1)
    while surplus > 0:
        free = [i for i in range(count - 1) if counts[i] < bound]
        pool, remaining = sum([portions[i] for i in free]), surplus
        for i in free:
            addition = min(bound - counts[i], max(1, remaining * portions[i] // pool), surplus)
            counts[i] = counts[i] + addition
            surplus = surplus - addition
    return np.array([bound] + counts)


def ragged_sizes(stream_key, amount, total, limit, slope):
    if amount == 2:
        one = jax.random.randint(stream_key, (), max(1, total - limit), min(limit, total - 1) + 1)
        return jnp.stack([one, total - one])
    tallies = jnp.asarray(profile(amount, total, limit, slope), jnp.int32)
    couples = (amount - 1) // 2
    donor, taker = tallies[1:1 + 2 * couples:2], tallies[2:2 + 2 * couples:2]
    margin = jnp.minimum(donor - 1, limit - taker)
    shifted = jax.random.randint(jax.random.fold_in(stream_key, 1), (couples,), 0, 1 << 20) % (margin + 1)
    tallies = tallies.at[1:1 + 2 * couples:2].set(donor - shifted).at[2:2 + 2 * couples:2].set(taker + shifted)
    return tallies[jax.random.permutation(jax.random.fold_in(stream_key, 2), amount)]


def gaussian(own_key, extent, width, limit, cuts=(), kind=jnp.bfloat16):
    loudness = level_of(own_key, extent, cuts, -0.22, 0.18) if cuts else 1.0
    result = jax.random.normal(own_key, extent, jnp.float32) * width * loudness
    return jnp.minimum(jnp.maximum(result, -limit), limit).astype(kind)


def setup_inputs(seed: int = 0) -> dict:
    streams_of = jax.random.split(jax.random.key(seed), 10)
    ends_in = draw_ends_in(jax.random.fold_in(streams_of[9], 71), 0)
    segments = jax.vmap(lambda own: jnp.searchsorted(jnp.cumsum(ragged_sizes(own, 8, LEN, LEN // 4, 1)), jnp.arange(LEN), side="right"))(jax.random.split(streams_of[1], NSEQ)).reshape((NSEQ, LEN)).astype(jnp.int32)
    qkv_weight = draw_qkv_weight(jax.random.fold_in(streams_of[9], 71), 0)
    out_weight = gaussian(streams_of[3], (2, D, D), (D // 32) ** -0.5, 1.0, ((0, 2), (1, 4)))
    up_weight = gaussian(streams_of[4], (2, D, FF), D ** -0.5, 0.1875, ((0, 2), (1, 4)))
    down_weight = gaussian(streams_of[5], (2, FF, D), FF ** -0.5, 0.09375, ((0, 2), (1, 4)))
    gains = jnp.clip(1.0 + 0.1 * jax.random.normal(streams_of[6], (2, 2, D), jnp.float32), 0.5, 1.5).astype(jnp.bfloat16)
    shifts = gaussian(streams_of[7], (2, 6, D), 0.5, 3.0, ((0, 2), (2, 4)))
    up_bias = gaussian(streams_of[8], (2, FF), 0.5, 3.0, ((0, 2), (1, 4)))
    return dict(ends_in=ends_in, segments=segments, qkv_weight=qkv_weight, out_weight=out_weight, up_weight=up_weight, down_weight=down_weight, gains=gains, shifts=shifts, up_bias=up_bias)


EPSILON = 1e-05
MASKED = -1e+30

def layer_norm(row_values, gain_vec, shift_vec):
    center = row_values - lax.optimization_barrier(jnp.mean(row_values, axis=-1, keepdims=True))
    spread = lax.optimization_barrier(jnp.mean(center * center, axis=-1, keepdims=True))
    return center * lax.rsqrt(spread + EPSILON) * gain_vec + shift_vec

def smooth_gate(upper_act):
    return jax.nn.gelu(upper_act, approximate=True)

def section_params(layer, qkv_weight, out_weight, up_weight, down_weight, gains, shifts, up_bias):
    return (qkv_weight[layer], out_weight[layer], up_weight[layer], down_weight[layer], gains[layer].astype(jnp.float32), shifts[layer].astype(jnp.float32), up_bias[layer].astype(jnp.float32))

def masked_scores(query_block, key_heads, full_segments, offset):
    block_rows = query_block.shape[0]
    raw_scores = jnp.einsum('qhd,khd->hqk', query_block.astype(jnp.float32), key_heads.astype(jnp.float32)) * DH ** (-0.5)
    query_pos = offset + jnp.arange(block_rows, dtype=jnp.int32)
    key_pos = jnp.arange(key_heads.shape[0], dtype=jnp.int32)
    query_segments = lax.dynamic_slice_in_dim(full_segments, offset, block_rows, 0)
    allowed = (key_pos[None, :] <= query_pos[:, None]) & (query_segments[:, None] == full_segments[None, :])
    return jnp.where(allowed[None], raw_scores, MASKED)

def attention(query_heads, key_heads, value_heads, full_segments):
    length = query_heads.shape[0]
    block_rows = min(512, length)
    block_count = length // block_rows

    def one_block(block_index):
        offset = block_index * block_rows
        query_block = lax.dynamic_slice_in_dim(query_heads, offset, block_rows, 0)
        scores = masked_scores(query_block, key_heads, full_segments, offset)
        row_max = lax.optimization_barrier(jnp.max(scores, axis=-1, keepdims=True))
        log_total = jnp.log(lax.optimization_barrier(jnp.sum(jnp.exp(scores - row_max), axis=-1, keepdims=True))) + row_max
        weights_block = jnp.exp(scores - log_total).astype(jnp.bfloat16)
        block_out = jnp.einsum('hqk,khd->qhd', weights_block.astype(jnp.float32), value_heads.astype(jnp.float32)).astype(jnp.bfloat16)
        return (block_out, log_total[..., 0])
    block_outs, totals = lax.map(one_block, jnp.arange(block_count, dtype=jnp.int32))
    return (block_outs.reshape(length, H, DH), jnp.moveaxis(totals, 0, 1).reshape(H, length))

def attention_grad(query_heads, key_heads, value_heads, attended, log_totals, grads_in, full_segments):
    length = query_heads.shape[0]
    block_rows = min(512, length)
    block_count = length // block_rows
    score_scale = DH ** (-0.5)
    row_delta = jnp.transpose(lax.optimization_barrier(jnp.sum(grads_in.astype(jnp.float32) * attended.astype(jnp.float32), axis=-1)))

    def one_block(carried, block_index):
        keys_grad, values_grad = carried
        offset = block_index * block_rows
        query_block = lax.dynamic_slice_in_dim(query_heads, offset, block_rows, 0)
        grad_block = lax.dynamic_slice_in_dim(grads_in, offset, block_rows, 0)
        scores = masked_scores(query_block, key_heads, full_segments, offset)
        weights_block = jnp.exp(scores - lax.dynamic_slice_in_dim(log_totals, offset, block_rows, 1)[..., None])
        weights_round = weights_block.astype(jnp.bfloat16)
        values_grad = values_grad + jnp.einsum('hqk,qhd->khd', weights_round.astype(jnp.float32), grad_block.astype(jnp.float32))
        weights_grad = jnp.einsum('qhd,khd->hqk', grad_block.astype(jnp.float32), value_heads.astype(jnp.float32))
        delta_block = lax.dynamic_slice_in_dim(row_delta, offset, block_rows, 1)[..., None]
        scores_grad = (weights_block * (weights_grad - delta_block)).astype(jnp.bfloat16)
        query_grad = jnp.einsum('hqk,khd->qhd', scores_grad.astype(jnp.float32), key_heads.astype(jnp.float32)) * score_scale
        keys_grad = keys_grad + jnp.einsum('hqk,qhd->khd', scores_grad.astype(jnp.float32), query_block.astype(jnp.float32)) * score_scale
        return ((keys_grad, values_grad), query_grad.astype(jnp.bfloat16))
    zero_grad = jnp.zeros(key_heads.shape, jnp.float32)
    (keys_grad, values_grad), query_parts = lax.scan(one_block, (zero_grad, zero_grad), jnp.arange(block_count, dtype=jnp.int32))
    return (query_parts.reshape(length, H, DH), keys_grad.astype(jnp.bfloat16), values_grad.astype(jnp.bfloat16))

def layer_forward(entry_rows, full_segments, params):
    qkv_w, out_w, up_w, down_w, gain_vecs, shift_vecs, up_vec = params
    length = entry_rows.shape[0]
    row_values = entry_rows.astype(jnp.float32)
    normed = layer_norm(row_values, gain_vecs[0], shift_vecs[0]).astype(jnp.bfloat16)
    qkv_bias = jnp.concatenate([shift_vecs[1], jnp.zeros((D,), jnp.float32), shift_vecs[2]])
    projected = (jnp.dot(normed, qkv_w, preferred_element_type=jnp.float32) + qkv_bias).astype(jnp.bfloat16)
    split_view = projected.reshape(length, 3, H, DH)
    query_heads, key_heads, value_heads = (split_view[:, 0], split_view[:, 1], split_view[:, 2])
    attended, log_totals = attention(query_heads, key_heads, value_heads, full_segments)
    flat_attended = attended.reshape(length, D)
    residual = row_values + jnp.dot(flat_attended, out_w, preferred_element_type=jnp.float32) + shift_vecs[3]
    normed_two = layer_norm(residual, gain_vecs[1], shift_vecs[4]).astype(jnp.bfloat16)
    upper_act = jnp.dot(normed_two, up_w, preferred_element_type=jnp.float32) + up_vec
    hidden = smooth_gate(upper_act).astype(jnp.bfloat16)
    output = residual + jnp.dot(hidden, down_w, preferred_element_type=jnp.float32) + shift_vecs[5]
    saved = (normed, query_heads, key_heads, value_heads, attended, log_totals, residual, normed_two, upper_act, hidden)
    return (saved, output)

def layer_backward(incoming, entry_rows, full_segments, saved, params):
    qkv_w, out_w, up_w, down_w, gain_vecs, shift_vecs, up_vec = params
    normed, query_heads, key_heads, value_heads, attended, log_totals, residual, normed_two, upper_act, hidden = saved
    length = entry_rows.shape[0]
    upstream = incoming.astype(jnp.float32)
    down_g = jnp.dot(hidden.astype(jnp.float32).T, upstream, precision=lax.Precision.HIGHEST)
    down_bias_g = lax.optimization_barrier(jnp.sum(upstream, axis=0))
    hidden_g = jnp.dot(upstream, down_w.astype(jnp.float32).T, precision=lax.Precision.HIGHEST)
    upper_g = jax.vjp(smooth_gate, upper_act)[1](hidden_g)[0]
    upper_round = upper_g.astype(jnp.bfloat16)
    up_g = jnp.dot(normed_two.astype(jnp.float32).T, upper_round.astype(jnp.float32), precision=lax.Precision.HIGHEST)
    up_bias_g = lax.optimization_barrier(jnp.sum(upper_g, axis=0))
    normed_two_g = jnp.dot(upper_round.astype(jnp.float32), up_w.astype(jnp.float32).T, precision=lax.Precision.HIGHEST)
    norm_back = jax.vjp(layer_norm, residual, gain_vecs[1], shift_vecs[4])[1]
    residual_part, gain_two_g, shift_two_g = norm_back(normed_two_g)
    residual_g = upstream + residual_part
    residual_round = residual_g.astype(jnp.bfloat16)
    flat_attended = attended.reshape(length, D)
    out_g = jnp.dot(flat_attended.astype(jnp.float32).T, residual_round.astype(jnp.float32), precision=lax.Precision.HIGHEST)
    out_bias_g = lax.optimization_barrier(jnp.sum(residual_g, axis=0))
    attended_g = jnp.dot(residual_round.astype(jnp.float32), out_w.astype(jnp.float32).T, precision=lax.Precision.HIGHEST).astype(jnp.bfloat16)
    query_g, keys_g, values_g = attention_grad(query_heads, key_heads, value_heads, attended, log_totals, attended_g.reshape(length, H, DH), full_segments)
    joined = jnp.concatenate([query_g.reshape(length, D), keys_g.reshape(length, D), values_g.reshape(length, D)], axis=1)
    qkv_g = jnp.dot(normed.astype(jnp.float32).T, joined.astype(jnp.float32), precision=lax.Precision.HIGHEST)
    column_sums = lax.optimization_barrier(jnp.sum(joined.astype(jnp.float32), axis=0))
    normed_g = jnp.dot(joined.astype(jnp.float32), qkv_w.astype(jnp.float32).T, precision=lax.Precision.HIGHEST)
    entry_back = jax.vjp(layer_norm, entry_rows.astype(jnp.float32), gain_vecs[0], shift_vecs[0])[1]
    entry_part, gain_one_g, shift_one_g = entry_back(normed_g)
    entry_g = residual_g + entry_part
    gains_g = jnp.stack([gain_one_g, gain_two_g])
    shifts_g = jnp.stack([shift_one_g, column_sums[:D], column_sums[2 * D:], out_bias_g, shift_two_g, down_bias_g])
    return ((qkv_g, out_g, up_g, down_g, gains_g, shifts_g, up_bias_g), entry_g)

def reference(ends_in, segments, qkv_weight, out_weight, up_weight, down_weight, gains, shifts, up_bias):
    first_layer = section_params(0, qkv_weight, out_weight, up_weight, down_weight, gains, shifts, up_bias)
    second_layer = section_params(1, qkv_weight, out_weight, up_weight, down_weight, gains, shifts, up_bias)

    def one_sequence(totals, item):
        entry_rows, incoming, full_segments = item
        saved_first, output_first = layer_forward(entry_rows, full_segments, first_layer)
        middle = output_first.astype(jnp.bfloat16)
        saved_second, output_second = layer_forward(middle, full_segments, second_layer)
        grads_second, middle_g = layer_backward(incoming, middle, full_segments, saved_second, second_layer)
        grads_first, entry_g = layer_backward(middle_g.astype(jnp.bfloat16), entry_rows, full_segments, saved_first, first_layer)
        totals = jax.tree.map(lambda acc, one_g, two_g: acc + jnp.stack([one_g, two_g]), totals, grads_first, grads_second)
        return (totals, (entry_g, output_second))
    start_totals = tuple((jnp.zeros(weight.shape, jnp.float32) for weight in (qkv_weight, out_weight, up_weight, down_weight, gains, shifts, up_bias)))
    totals, (entry_grads, outputs) = lax.scan(one_sequence, start_totals, (ends_in[0], ends_in[1], segments))
    ends_out = jnp.stack([entry_grads, outputs])
    return (ends_out, totals[0], totals[1], totals[2], totals[3], totals[4], totals[5], totals[6])
```

```python
import jax
import jax.numpy as jnp
from jax import lax
from jax.experimental import pallas as pl
from jax.experimental.pallas import tpu as pltpu
from jax.sharding import PartitionSpec as P

DH = 64


EPSILON = 1e-05
MASKED = -1e30


def passed_along(array, axis, by):
    count = lax.axis_size(axis)
    pairs = [(i, i + by) for i in range(count) if 0 <= i + by < count]
    return lax.ppermute(array, axis, pairs)


def layer_norm(row_values, gain_vec, shift_vec):
    center = row_values - jnp.mean(row_values, axis=-1, keepdims=True)
    spread = jnp.mean(center * center, axis=-1, keepdims=True)
    return center * lax.rsqrt(spread + EPSILON) * gain_vec + shift_vec


def smooth_gate(upper_act):
    return jax.nn.gelu(upper_act, approximate=True)


def halo_chunks():
    return max(1, lax.axis_size("seq") // 4)


def from_before(array):
    return jnp.stack([passed_along(array, "seq", by) for by in range(halo_chunks(), 0, -1)])


def score_bias(segments):
    chunks = halo_chunks()
    tok_count = segments.shape[1]
    place = lax.axis_index("seq")
    before = from_before(segments)
    window = [
        jnp.where(place >= chunks - chunk, before[chunk], -1) for chunk in range(chunks)
    ] + [segments]
    keys = jnp.concatenate(window, axis=1)
    query_pos = lax.iota(jnp.int32, tok_count) + chunks * tok_count
    key_pos = lax.iota(jnp.int32, keys.shape[1])
    allowed = (key_pos[None, :] <= query_pos[:, None])[None]
    allowed = allowed & (keys[:, None, :] == segments[:, :, None])
    return jnp.where(allowed, 0.0, MASKED).astype(jnp.float32)


def halves_of(pair):
    lane = lax.broadcasted_iota(jnp.int32, pair.shape, 1)
    low = jnp.where(lane < DH, pair, jnp.zeros_like(pair))
    high = jnp.where(lane < DH, jnp.zeros_like(pair), pair)
    return jnp.concatenate([low, high], axis=0)


def joined_halves(stacked):
    tok_count = stacked.shape[0] // 2
    low, high = stacked[:tok_count], stacked[tok_count:]
    return jnp.where(lax.broadcasted_iota(jnp.int32, low.shape, 1) < DH, low, high)


def dot_last(left, right):
    return lax.dot_general(
        left, right, (((1,), (1,)), ((), ())), preferred_element_type=jnp.float32
    )


def dot_first(left, right):
    return lax.dot_general(
        left, right, (((0,), (0,)), ((), ())), preferred_element_type=jnp.float32
    )


def pair_scores(query_pair, key_pair, bias):
    scores = dot_last(halves_of(query_pair), key_pair) * DH ** (-0.5)
    scores = scores + jnp.concatenate([bias, bias], axis=0)
    row_max = jnp.max(scores, axis=-1, keepdims=True)
    log_total = jnp.log(jnp.sum(jnp.exp(scores - row_max), axis=-1, keepdims=True)) + row_max
    return jnp.exp(scores - log_total)


def window_pair(halo_ref, own_ref, rows, first):
    columns = pl.ds(first, 2 * DH)
    parts = [halo_ref[chunk, rows, columns] for chunk in range(halo_ref.shape[0])]
    return jnp.concatenate(parts + [own_ref[rows, columns]], axis=0)


def attend_kernel(query_ref, own_ref, halo_ref, bias_ref, out_ref):
    tok_count, width = bias_ref.shape[1], query_ref.shape[1]
    for sequence in range(bias_ref.shape[0]):
        rows = pl.ds(sequence * tok_count, tok_count)
        bias = bias_ref[sequence]
        for first in range(0, width, 2 * DH):
            weights = pair_scores(
                query_ref[rows, pl.ds(first, 2 * DH)],
                window_pair(halo_ref, own_ref, rows, first),
                bias,
            )
            values = window_pair(halo_ref, own_ref, rows, width + first)
            attended = jnp.dot(
                weights.astype(jnp.bfloat16), values, preferred_element_type=jnp.float32
            )
            out_ref[rows, pl.ds(first, 2 * DH)] = joined_halves(attended).astype(jnp.bfloat16)


def attend_grad_kernel(
    query_ref, own_ref, halo_ref, bias_ref, out_ref, grad_ref, query_g_ref, own_g_ref, halo_g_ref
):
    tok_count, width = bias_ref.shape[1], query_ref.shape[1]
    chunks = halo_ref.shape[0]
    for sequence in range(bias_ref.shape[0]):
        rows = pl.ds(sequence * tok_count, tok_count)
        bias = bias_ref[sequence]
        for first in range(0, width, 2 * DH):
            columns = pl.ds(first, 2 * DH)
            query_pair, grad_pair = query_ref[rows, columns], grad_ref[rows, columns]
            keys = window_pair(halo_ref, own_ref, rows, first)
            values = window_pair(halo_ref, own_ref, rows, width + first)
            weights = pair_scores(query_pair, keys, bias)
            queries_two, grads_two = halves_of(query_pair), halves_of(grad_pair)
            products = grads_two.astype(jnp.float32) * halves_of(out_ref[rows, columns]).astype(
                jnp.float32
            )
            row_delta = jnp.sum(products, axis=-1, keepdims=True)
            scores_g = (weights * (dot_last(grads_two, values) - row_delta)).astype(jnp.bfloat16)
            query_g = jnp.dot(scores_g, keys, preferred_element_type=jnp.float32)
            query_g_ref[rows, columns] = (joined_halves(query_g) * DH ** (-0.5)).astype(
                jnp.bfloat16
            )
            keys_g = dot_first(scores_g, queries_two) * DH ** (-0.5)
            values_g = dot_first(weights.astype(jnp.bfloat16), grads_two)
            for grad, start in ((keys_g, first), (values_g, width + first)):
                for chunk in range(chunks):
                    halo_g_ref[chunk, rows, pl.ds(start, 2 * DH)] = grad[
                        chunk * tok_count : (chunk + 1) * tok_count
                    ].astype(jnp.bfloat16)
                own_g_ref[rows, pl.ds(start, 2 * DH)] = grad[chunks * tok_count :]


def in_vmem(count):
    return [pl.BlockSpec(memory_space=pltpu.VMEM)] * count


def attend(query, own, halo, bias):
    return pl.pallas_call(
        attend_kernel,
        out_shape=jax.ShapeDtypeStruct(query.shape, jnp.bfloat16),
        in_specs=in_vmem(4),
        out_specs=pl.BlockSpec(memory_space=pltpu.VMEM),
        cost_estimate=pl.CostEstimate(flops=10**9, bytes_accessed=10**7, transcendentals=0),
        name="attend",
    )(query, own, halo, bias)


def attend_grad(query, own, halo, bias, attended, heads_grad):
    return pl.pallas_call(
        attend_grad_kernel,
        out_shape=(
            jax.ShapeDtypeStruct(query.shape, jnp.bfloat16),
            jax.ShapeDtypeStruct(own.shape, jnp.float32),
            jax.ShapeDtypeStruct(halo.shape, jnp.bfloat16),
        ),
        in_specs=in_vmem(6),
        out_specs=tuple(in_vmem(3)),
        cost_estimate=pl.CostEstimate(flops=10**9, bytes_accessed=10**7, transcendentals=0),
        name="attend_grad",
    )(query, own, halo, bias, attended, heads_grad)


def forward(entry_rows, params, bias):
    qkv_w, out_w, up_w, down_w, gain_vecs, vectors, up_vec = params
    width = entry_rows.shape[-1]
    row_values = entry_rows.reshape(-1, width).astype(jnp.float32)
    normed = layer_norm(row_values, gain_vecs[0], vectors[0]).astype(jnp.bfloat16)
    own_bias = jnp.concatenate([jnp.zeros_like(vectors[2]), vectors[2]])
    own = jnp.dot(normed, qkv_w[:, width:], preferred_element_type=jnp.float32) + own_bias
    own = own.astype(jnp.bfloat16)
    halo = from_before(own)
    query = jnp.dot(normed, qkv_w[:, :width], preferred_element_type=jnp.float32) + vectors[1]
    query = query.astype(jnp.bfloat16)
    mixed = attend(query, own, halo, bias)
    residual = row_values + jnp.dot(mixed, out_w, preferred_element_type=jnp.float32) + vectors[3]
    normed_two = layer_norm(residual, gain_vecs[1], vectors[4]).astype(jnp.bfloat16)
    upper_act = jnp.dot(normed_two, up_w, preferred_element_type=jnp.float32) + up_vec
    hidden = smooth_gate(upper_act).astype(jnp.bfloat16)
    output = residual + jnp.dot(hidden, down_w, preferred_element_type=jnp.float32) + vectors[5]
    return (output, (normed, query, own, halo, mixed, residual, normed_two, upper_act))


def backward(incoming, entry_rows, params, saved, bias, beside=None):
    qkv_w, out_w, up_w, down_w, gain_vecs, vectors, up_vec = params
    normed, query, own, halo, mixed, residual, normed_two, upper_act = saved
    width = entry_rows.shape[-1]
    grad_rows = incoming.reshape(-1, width)
    upstream = grad_rows.astype(jnp.float32)
    down_bias_g = jnp.sum(upstream, axis=0)
    hidden_g = jnp.einsum("rd,fd->rf", grad_rows, down_w, preferred_element_type=jnp.float32)
    upper_g = jax.vjp(smooth_gate, upper_act)[1](hidden_g)[0]
    up_bias_g = jnp.sum(upper_g, axis=0)
    normed_two_g = jnp.einsum(
        "rf,df->rd", upper_g.astype(jnp.bfloat16), up_w, preferred_element_type=jnp.float32
    )
    norm_back = jax.vjp(layer_norm, residual, gain_vecs[1], vectors[4])[1]
    residual_part, gain_two_g, shift_two_g = norm_back(normed_two_g)
    residual_g = upstream + residual_part
    residual_round = residual_g.astype(jnp.bfloat16)
    out_bias_g = jnp.sum(residual_g, axis=0)
    mixed_g = jnp.einsum(
        "re,de->rd", residual_round, out_w, preferred_element_type=jnp.float32
    ).astype(jnp.bfloat16)
    query_g, own_g, halo_g = attend_grad(query, own, halo, bias, mixed, mixed_g)
    if beside is not None:
        query_g, halo_g, beside = lax.optimization_barrier((query_g, halo_g, beside))
    chunks = halo_g.shape[0]
    for chunk in range(chunks):
        own_g = own_g + passed_along(halo_g[chunk], "seq", chunk - chunks).astype(jnp.float32)
    own_g = own_g.astype(jnp.bfloat16)
    column_sums = jnp.sum(query_g.astype(jnp.float32), axis=0)
    value_sums = jnp.sum(own_g[:, width:].astype(jnp.float32), axis=0)
    normed_g = jnp.einsum(
        "re,de->rd", query_g, qkv_w[:, :width], preferred_element_type=jnp.float32
    ) + jnp.einsum("re,de->rd", own_g, qkv_w[:, width:], preferred_element_type=jnp.float32)
    row_values = entry_rows.reshape(-1, width).astype(jnp.float32)
    entry_back = jax.vjp(layer_norm, row_values, gain_vecs[0], vectors[0])[1]
    entry_part, gain_one_g, shift_one_g = entry_back(normed_g)
    vector_grads = (
        jnp.stack([gain_one_g, gain_two_g]),
        jnp.stack(
            [shift_one_g, column_sums, value_sums, out_bias_g, shift_two_g, down_bias_g]
        ),
        up_bias_g[None],
    )
    joined = jnp.concatenate([query_g, own_g], axis=1)
    return (residual_g + entry_part, residual_round, joined, vector_grads, beside)


def rounded_blocks(partial):
    owners = lax.axis_size("dp")
    return partial.reshape(owners, -1, partial.shape[1]).astype(jnp.bfloat16)


def summed_blocks(blocks):
    return lax.psum_scatter(
        blocks.reshape(-1, blocks.shape[2]), "dp", scatter_dimension=0, tiled=True
    )


def gathered_parts(own):
    return lax.all_gather(own, "seq", axis=0, tiled=False)


def own_columns(array, outer, inner):
    index = lax.axis_index("seq")
    rows = array.shape[0]
    parts = array.reshape(rows, outer, inner, -1)
    return lax.dynamic_index_in_dim(parts, index, 2, keepdims=False).reshape(rows, -1)


def own_rows(array, outer, inner):
    index = lax.axis_index("seq")
    columns = array.shape[1]
    parts = array.reshape(outer, inner, -1, columns)
    return lax.dynamic_index_in_dim(parts, index, 1, keepdims=False).reshape(-1, columns)


def feed_forward_grads(normed_two, incoming, params):
    up_w, down_w, up_vec = params[2], params[3], params[6]
    outer, inner = lax.axis_size("dp"), lax.axis_size("seq")
    up_part = own_columns(up_w, outer, inner)
    down_part = own_rows(down_w, outer, inner)
    bias_part = own_columns(up_vec[None], outer, inner)[0]
    upper_act = jnp.dot(normed_two, up_part, preferred_element_type=jnp.float32) + bias_part
    hidden_f, gate_back = jax.vjp(smooth_gate, upper_act)
    hidden = hidden_f.astype(jnp.bfloat16)
    hidden_g = jnp.einsum("rd,fd->rf", incoming, down_part, preferred_element_type=jnp.float32)
    upper_round = gate_back(hidden_g)[0].astype(jnp.bfloat16)
    down_g = jnp.einsum("rf,rd->fd", hidden, incoming, preferred_element_type=jnp.float32)
    up_g = jnp.einsum("rd,rf->df", normed_two, upper_round, preferred_element_type=jnp.float32)
    return (up_g, down_g)


def joined_columns(parts, outer_columns):
    inner, rows, columns = parts.shape
    ordered = parts.reshape(inner, rows, outer_columns, -1).transpose(1, 2, 0, 3)
    return ordered.reshape(rows, inner * columns).astype(jnp.float32)


def gathered_rows(values):
    return lax.all_gather(values, "seq", axis=0, tiled=True)


def by_owner(array, owners):
    rows, columns = array.shape
    return array.reshape(rows, owners, -1).transpose(1, 0, 2).reshape(owners, -1)


def piece_plan(shapes):
    return [
        (which, part * (rows // (2 * pieces)), rows // (2 * pieces), rows // 2)
        for which, (rows, columns) in enumerate(shapes)
        for pieces in (2 if rows * columns > 512 * 1024 else 1,)
        for part in range(pieces)
    ]


def gather_kernel(plan, count, *refs):
    own, full = refs[:count], refs[count : 2 * count]
    (local_sem, own_send, own_recv, far_send, far_recv) = refs[2 * count : 2 * count + 5]
    (side_send, side_recv, near_send, near_recv, last_send, last_recv) = refs[2 * count + 5 :]
    me, place = lax.axis_index("dp"), lax.axis_index("seq")
    far = lax.rem(me + 2, 4)
    near = me + 1 - 2 * lax.rem(me, 2)
    half = lax.rem(place, 2)
    side = place + 1 - 2 * half
    barrier = pltpu.get_barrier_semaphore()
    for target in ({"dp": far}, {"dp": near}, {"seq": side}):
        pl.semaphore_signal(
            barrier, inc=1, device_id=target, device_id_type=pl.DeviceIdType.MESH
        )
    pl.semaphore_wait(barrier, 3)

    def rows_at(which_half, first, rows, half_rows):
        return pl.ds(pl.multiple_of(which_half * half_rows + first, rows), rows)

    def remote(source, target, send, recv, device):
        return pltpu.make_async_remote_copy(
            src_ref=source,
            dst_ref=target,
            send_sem=send,
            recv_sem=recv,
            device_id=device,
            device_id_type=pl.DeviceIdType.MESH,
        )

    far_copies, side_copies, near_copies, last_copies = [], [], [], []
    for index, (which, first, rows, half_rows) in enumerate(plan):
        span = rows_at(half, first, rows, half_rows)
        copy = remote(
            own[which].at[span],
            full[which].at[me, span],
            far_send.at[index],
            far_recv.at[index],
            {"dp": far},
        )
        copy.start()
        far_copies.append(copy)
    own_copies, local_copies = [], []
    for which in range(count):
        copy = remote(
            own[which], full[which].at[me], own_send.at[which], own_recv.at[which], {"dp": near}
        )
        copy.start()
        own_copies.append(copy)
        copy = pltpu.make_async_copy(own[which], full[which].at[me], local_sem.at[which])
        copy.start()
        local_copies.append(copy)

    def last_step(index):
        which, first, rows, half_rows = plan[index]
        side_copies[index].wait_recv()
        block = full[which].at[far, rows_at(1 - half, first, rows, half_rows)]
        copy = remote(block, block, last_send.at[index], last_recv.at[index], {"dp": near})
        copy.start()
        last_copies.append(copy)

    for index, (which, first, rows, half_rows) in enumerate(plan):
        far_copies[index].wait_recv()
        block = full[which].at[far, rows_at(half, first, rows, half_rows)]
        copy = remote(block, block, side_send.at[index], side_recv.at[index], {"seq": side})
        copy.start()
        side_copies.append(copy)
        copy = remote(block, block, near_send.at[index], near_recv.at[index], {"dp": near})
        copy.start()
        near_copies.append(copy)
        if index > 0:
            last_step(index - 1)
    last_step(len(plan) - 1)
    for copy in near_copies + last_copies + own_copies:
        copy.wait_recv()
    for copy in far_copies + side_copies + near_copies + last_copies + own_copies:
        copy.wait_send()
    for copy in local_copies:
        copy.wait()


def gathered_weights(weights):
    owners, places = lax.axis_size("dp"), lax.axis_size("seq")
    if owners != 4 or places % 2:
        return [lax.all_gather(weight, "dp", axis=0, tiled=True) for weight in weights]
    plan = piece_plan([weight.shape for weight in weights])
    count, pieces = len(weights), len(plan)
    dma = pltpu.SemaphoreType.DMA
    full = pl.pallas_call(
        lambda *refs: gather_kernel(plan, count, *refs),
        out_shape=[jax.ShapeDtypeStruct((owners,) + w.shape, w.dtype) for w in weights],
        in_specs=[pl.BlockSpec(memory_space=pltpu.VMEM)] * count,
        out_specs=[pl.BlockSpec(memory_space=pl.ANY)] * count,
        scratch_shapes=[dma((count,))] * 3 + [dma((pieces,))] * 8,
        compiler_params=pltpu.CompilerParams(collective_id=0, has_side_effects=True),
        name="gather_weights",
    )(*weights)
    return [whole.reshape(-1, whole.shape[2]) for whole in full]


def shards(
    ends_in, segments, qkv_weight, out_weight, up_weight, down_weight, gains, shifts, up_bias
):
    section_index = lax.axis_index("section")
    leading = section_index == 0
    outer, inner = lax.axis_size("dp"), lax.axis_size("seq")
    own_slot = ends_in[0]
    seq_count, tok_count, width = own_slot.shape
    share = width // outer
    packed = jnp.concatenate([gains[0].reshape(-1), shifts[0].reshape(-1), up_bias[0]])
    packed = lax.all_gather(packed, "dp", axis=0, tiled=False).astype(jnp.float32)
    gain_count, shift_count = gains.shape[1], shifts.shape[1]

    def rows_of(first, count):
        part = packed[:, first * share : (first + count) * share]
        return part.reshape(outer, count, share).transpose(1, 0, 2).reshape(count, width)

    params = (
        *gathered_weights((qkv_weight[0], out_weight[0], up_weight[0], down_weight[0])),
        rows_of(0, gain_count),
        rows_of(gain_count, shift_count),
        packed[:, (gain_count + shift_count) * share :].reshape(-1),
    )
    bias = score_bias(segments)

    first_output = forward(own_slot, params, bias)[0]
    received = passed_along(
        first_output.astype(jnp.bfloat16).reshape(own_slot.shape), "section", 1
    )
    entry_rows = jnp.where(leading, own_slot, received)
    last_output, saved = forward(entry_rows, params, bias)
    normed, query, own, halo, mixed, residual, normed_two, upper_act = saved
    tokens_in = gathered_rows(jnp.concatenate([normed, normed_two, mixed], axis=1))
    early_entry = backward(own_slot, entry_rows, params, saved, bias)[0]
    early_entry, tokens_in = lax.optimization_barrier((early_entry, tokens_in))
    all_normed = tokens_in[:, :width]
    all_normed_two = tokens_in[:, width : 2 * width]
    all_mixed = tokens_in[:, 2 * width :]
    returned = passed_along(
        early_entry.astype(jnp.bfloat16).reshape(own_slot.shape), "section", -1
    )
    incoming = jnp.where(leading, returned, own_slot)
    all_incoming = gathered_rows(incoming.reshape(-1, width))
    up_g, down_g = feed_forward_grads(all_normed_two, all_incoming, params)
    up_columns = up_g.shape[1]
    gate_blocks = jnp.concatenate(
        [rounded_blocks(up_g), rounded_blocks(down_g.reshape(width, -1))], axis=2
    )
    entry_g, residual_round, joined_heads, vector_grads, gate_blocks = backward(
        incoming, entry_rows, params, saved, bias, gate_blocks
    )
    gate_own = summed_blocks(gate_blocks)
    sent = jnp.concatenate(
        [
            joined_heads.reshape(-1, inner, 3 * width // inner),
            residual_round.reshape(-1, inner, width // inner),
        ],
        axis=2,
    )
    sent = lax.all_to_all(sent, "seq", split_axis=1, concat_axis=0, tiled=True)
    sent = sent.reshape(-1, sent.shape[2])
    joined_part, residual_part = sent[:, : 3 * width // inner], sent[:, 3 * width // inner :]
    out_g = jnp.einsum("rd,re->de", all_mixed, residual_part, preferred_element_type=jnp.float32)
    qkv_g = jnp.einsum("rd,re->de", all_normed, joined_part, preferred_element_type=jnp.float32)
    matrix_part = jnp.concatenate([rounded_blocks(qkv_g), rounded_blocks(out_g)], axis=2)
    vectors_g = jnp.concatenate([by_owner(part, outer) for part in vector_grads], axis=1)
    columns, vector_size = matrix_part.shape[2], vectors_g.shape[1]
    vector_rows = -(-vector_size // (16 * columns)) * 16
    vectors_g = jnp.pad(vectors_g, ((0, 0), (0, vector_rows * columns - vector_size)))
    vectors_g = rounded_blocks(vectors_g.reshape(-1, columns))
    last_blocks = jnp.concatenate([matrix_part, vectors_g], axis=1)
    last_blocks, gate_own = lax.optimization_barrier((last_blocks, gate_own))
    gate_parts = gathered_parts(gate_own)
    last_own, gate_parts = lax.optimization_barrier((summed_blocks(last_blocks), gate_parts))
    up_total = joined_columns(gate_parts[:, :, :up_columns], outer)
    down_total = gate_parts[:, :, up_columns:].reshape(-1, width).astype(jnp.float32)
    parts = gathered_parts(last_own)
    qkv_columns = qkv_g.shape[1]
    qkv_total = joined_columns(parts[:, :share, :qkv_columns], 1)
    out_total = joined_columns(parts[:, :share, qkv_columns:], 1)
    own_vectors = jnp.sum(parts[:, share:].astype(jnp.float32), axis=0).reshape(-1)
    gains_total = own_vectors[: gain_count * share].reshape(gain_count, share)
    shifts_total = own_vectors[gain_count * share : (gain_count + shift_count) * share]
    shifts_total = shifts_total.reshape(shift_count, share)
    up_bias_total = own_vectors[(gain_count + shift_count) * share : vector_size]

    ends_out = jnp.where(leading, entry_g, last_output).reshape(own_slot.shape)[None]
    return (
        ends_out,
        qkv_total[None],
        out_total[None],
        up_total[None],
        down_total[None],
        gains_total[None],
        shifts_total[None],
        up_bias_total[None],
    )


def solution(mesh):
    in_specs = (
        P("section", "dp", "seq", None),
        P("dp", "seq"),
        P("section", "dp", None),
        P("section", "dp", None),
        P("section", "dp", None),
        P("section", "dp", None),
        P("section", None, "dp"),
        P("section", None, "dp"),
        P("section", "dp"),
    )
    out_specs = (
        P("section", "dp", "seq", None),
        P("section", "dp", None),
        P("section", "dp", None),
        P("section", "dp", None),
        P("section", "dp", None),
        P("section", None, "dp"),
        P("section", None, "dp"),
        P("section", "dp"),
    )
    return jax.shard_map(shards, mesh=mesh, in_specs=in_specs, out_specs=out_specs, check_vma=False)
```

```python
import jax
import jax.numpy as jnp
from jax import lax
from jax.experimental import pallas as pl
from jax.experimental.pallas import tpu as pltpu
from jax.sharding import PartitionSpec as P

DH = 64


EPSILON = 1e-05
MASKED = -1e30


def passed_along(array, axis, by):
    count = lax.axis_size(axis)
    pairs = [(i, i + by) for i in range(count) if 0 <= i + by < count]
    return lax.ppermute(array, axis, pairs)


def layer_norm(row_values, gain_vec, shift_vec):
    center = row_values - jnp.mean(row_values, axis=-1, keepdims=True)
    spread = jnp.mean(center * center, axis=-1, keepdims=True)
    return center * lax.rsqrt(spread + EPSILON) * gain_vec + shift_vec


def smooth_gate(upper_act):
    return jax.nn.gelu(upper_act, approximate=True)


def halo_chunks():
    return max(1, lax.axis_size("seq") // 4)


def from_before(array):
    return jnp.stack([passed_along(array, "seq", by) for by in range(halo_chunks(), 0, -1)])


def score_bias(segments):
    chunks = halo_chunks()
    tok_count = segments.shape[1]
    place = lax.axis_index("seq")
    before = from_before(segments)
    window = [
        jnp.where(place >= chunks - chunk, before[chunk], -1) for chunk in range(chunks)
    ] + [segments]
    keys = jnp.concatenate(window, axis=1)
    query_pos = lax.iota(jnp.int32, tok_count) + chunks * tok_count
    key_pos = lax.iota(jnp.int32, keys.shape[1])
    allowed = (key_pos[None, :] <= query_pos[:, None])[None]
    allowed = allowed & (keys[:, None, :] == segments[:, :, None])
    return jnp.where(allowed, 0.0, MASKED).astype(jnp.float32)


def halves_of(pair):
    lane = lax.broadcasted_iota(jnp.int32, pair.shape, 1)
    low = jnp.where(lane < DH, pair, jnp.zeros_like(pair))
    high = jnp.where(lane < DH, jnp.zeros_like(pair), pair)
    return jnp.concatenate([low, high], axis=0)


def joined_halves(stacked):
    tok_count = stacked.shape[0] // 2
    low, high = stacked[:tok_count], stacked[tok_count:]
    return jnp.where(lax.broadcasted_iota(jnp.int32, low.shape, 1) < DH, low, high)


def dot_last(left, right):
    return lax.dot_general(
        left, right, (((1,), (1,)), ((), ())), preferred_element_type=jnp.float32
    )


def dot_first(left, right):
    return lax.dot_general(
        left, right, (((0,), (0,)), ((), ())), preferred_element_type=jnp.float32
    )


def pair_scores(query_pair, key_pair, bias):
    scores = dot_last(halves_of(query_pair), key_pair) * DH ** (-0.5)
    scores = scores + jnp.concatenate([bias, bias], axis=0)
    row_max = jnp.max(scores, axis=-1, keepdims=True)
    log_total = jnp.log(jnp.sum(jnp.exp(scores - row_max), axis=-1, keepdims=True)) + row_max
    return jnp.exp(scores - log_total)


def window_pair(halo_ref, own_ref, rows, first):
    columns = pl.ds(first, 2 * DH)
    parts = [halo_ref[chunk, rows, columns] for chunk in range(halo_ref.shape[0])]
    return jnp.concatenate(parts + [own_ref[rows, columns]], axis=0)


def attend_kernel(query_ref, own_ref, halo_ref, bias_ref, out_ref):
    tok_count, width = bias_ref.shape[1], query_ref.shape[1]
    for sequence in range(bias_ref.shape[0]):
        rows = pl.ds(sequence * tok_count, tok_count)
        bias = bias_ref[sequence]
        for first in range(0, width, 2 * DH):
            weights = pair_scores(
                query_ref[rows, pl.ds(first, 2 * DH)],
                window_pair(halo_ref, own_ref, rows, first),
                bias,
            )
            values = window_pair(halo_ref, own_ref, rows, width + first)
            attended = jnp.dot(
                weights.astype(jnp.bfloat16), values, preferred_element_type=jnp.float32
            )
            out_ref[rows, pl.ds(first, 2 * DH)] = joined_halves(attended).astype(jnp.bfloat16)


def attend_grad_kernel(
    query_ref, own_ref, halo_ref, bias_ref, out_ref, grad_ref, query_g_ref, own_g_ref, halo_g_ref
):
    tok_count, width = bias_ref.shape[1], query_ref.shape[1]
    chunks = halo_ref.shape[0]
    for sequence in range(bias_ref.shape[0]):
        rows = pl.ds(sequence * tok_count, tok_count)
        bias = bias_ref[sequence]
        for first in range(0, width, 2 * DH):
            columns = pl.ds(first, 2 * DH)
            query_pair, grad_pair = query_ref[rows, columns], grad_ref[rows, columns]
            keys = window_pair(halo_ref, own_ref, rows, first)
            values = window_pair(halo_ref, own_ref, rows, width + first)
            weights = pair_scores(query_pair, keys, bias)
            queries_two, grads_two = halves_of(query_pair), halves_of(grad_pair)
            products = grads_two.astype(jnp.float32) * halves_of(out_ref[rows, columns]).astype(
                jnp.float32
            )
            row_delta = jnp.sum(products, axis=-1, keepdims=True)
            scores_g = (weights * (dot_last(grads_two, values) - row_delta)).astype(jnp.bfloat16)
            query_g = jnp.dot(scores_g, keys, preferred_element_type=jnp.float32)
            query_g_ref[rows, columns] = (joined_halves(query_g) * DH ** (-0.5)).astype(
                jnp.bfloat16
            )
            keys_g = dot_first(scores_g, queries_two) * DH ** (-0.5)
            values_g = dot_first(weights.astype(jnp.bfloat16), grads_two)
            for grad, start in ((keys_g, first), (values_g, width + first)):
                for chunk in range(chunks):
                    halo_g_ref[chunk, rows, pl.ds(start, 2 * DH)] = grad[
                        chunk * tok_count : (chunk + 1) * tok_count
                    ].astype(jnp.bfloat16)
                own_g_ref[rows, pl.ds(start, 2 * DH)] = grad[chunks * tok_count :]


def in_vmem(count):
    return [pl.BlockSpec(memory_space=pltpu.VMEM)] * count


def attend(query, own, halo, bias):
    return pl.pallas_call(
        attend_kernel,
        out_shape=jax.ShapeDtypeStruct(query.shape, jnp.bfloat16),
        in_specs=in_vmem(4),
        out_specs=pl.BlockSpec(memory_space=pltpu.VMEM),
        cost_estimate=pl.CostEstimate(flops=10**9, bytes_accessed=10**7, transcendentals=0),
        name="attend",
    )(query, own, halo, bias)


def attend_grad(query, own, halo, bias, attended, heads_grad):
    return pl.pallas_call(
        attend_grad_kernel,
        out_shape=(
            jax.ShapeDtypeStruct(query.shape, jnp.bfloat16),
            jax.ShapeDtypeStruct(own.shape, jnp.float32),
            jax.ShapeDtypeStruct(halo.shape, jnp.bfloat16),
        ),
        in_specs=in_vmem(6),
        out_specs=tuple(in_vmem(3)),
        cost_estimate=pl.CostEstimate(flops=10**9, bytes_accessed=10**7, transcendentals=0),
        name="attend_grad",
    )(query, own, halo, bias, attended, heads_grad)


def forward(entry_rows, params, bias):
    qkv_w, out_w, up_w, down_w, gain_vecs, vectors, up_vec = params
    width = entry_rows.shape[-1]
    row_values = entry_rows.reshape(-1, width).astype(jnp.float32)
    normed = layer_norm(row_values, gain_vecs[0], vectors[0]).astype(jnp.bfloat16)
    own_bias = jnp.concatenate([jnp.zeros_like(vectors[2]), vectors[2]])
    own = jnp.dot(normed, qkv_w[:, width:], preferred_element_type=jnp.float32) + own_bias
    own = own.astype(jnp.bfloat16)
    halo = from_before(own)
    query = jnp.dot(normed, qkv_w[:, :width], preferred_element_type=jnp.float32) + vectors[1]
    query = query.astype(jnp.bfloat16)
    mixed = attend(query, own, halo, bias)
    residual = row_values + jnp.dot(mixed, out_w, preferred_element_type=jnp.float32) + vectors[3]
    normed_two = layer_norm(residual, gain_vecs[1], vectors[4]).astype(jnp.bfloat16)
    upper_act = jnp.dot(normed_two, up_w, preferred_element_type=jnp.float32) + up_vec
    hidden = smooth_gate(upper_act).astype(jnp.bfloat16)
    output = residual + jnp.dot(hidden, down_w, preferred_element_type=jnp.float32) + vectors[5]
    return (output, (normed, query, own, halo, mixed, residual, normed_two, upper_act))


def backward(incoming, entry_rows, params, saved, bias):
    qkv_w, out_w, up_w, down_w, gain_vecs, vectors, up_vec = params
    normed, query, own, halo, mixed, residual, normed_two, upper_act = saved
    width = entry_rows.shape[-1]
    grad_rows = incoming.reshape(-1, width)
    upstream = grad_rows.astype(jnp.float32)
    down_bias_g = jnp.sum(upstream, axis=0)
    hidden_g = jnp.einsum("rd,fd->rf", grad_rows, down_w, preferred_element_type=jnp.float32)
    upper_g = jax.vjp(smooth_gate, upper_act)[1](hidden_g)[0]
    up_bias_g = jnp.sum(upper_g, axis=0)
    normed_two_g = jnp.einsum(
        "rf,df->rd", upper_g.astype(jnp.bfloat16), up_w, preferred_element_type=jnp.float32
    )
    norm_back = jax.vjp(layer_norm, residual, gain_vecs[1], vectors[4])[1]
    residual_part, gain_two_g, shift_two_g = norm_back(normed_two_g)
    residual_g = upstream + residual_part
    residual_round = residual_g.astype(jnp.bfloat16)
    out_bias_g = jnp.sum(residual_g, axis=0)
    mixed_g = jnp.einsum(
        "re,de->rd", residual_round, out_w, preferred_element_type=jnp.float32
    ).astype(jnp.bfloat16)
    query_g, own_g, halo_g = attend_grad(query, own, halo, bias, mixed, mixed_g)
    chunks = halo_g.shape[0]
    for chunk in range(chunks):
        own_g = own_g + passed_along(halo_g[chunk], "seq", chunk - chunks).astype(jnp.float32)
    own_g = own_g.astype(jnp.bfloat16)
    column_sums = jnp.sum(query_g.astype(jnp.float32), axis=0)
    value_sums = jnp.sum(own_g[:, width:].astype(jnp.float32), axis=0)
    normed_g = jnp.einsum(
        "re,de->rd", query_g, qkv_w[:, :width], preferred_element_type=jnp.float32
    ) + jnp.einsum("re,de->rd", own_g, qkv_w[:, width:], preferred_element_type=jnp.float32)
    row_values = entry_rows.reshape(-1, width).astype(jnp.float32)
    entry_back = jax.vjp(layer_norm, row_values, gain_vecs[0], vectors[0])[1]
    entry_part, gain_one_g, shift_one_g = entry_back(normed_g)
    vector_grads = (
        jnp.stack([gain_one_g, gain_two_g]),
        jnp.stack(
            [shift_one_g, column_sums, value_sums, out_bias_g, shift_two_g, down_bias_g]
        ),
        up_bias_g[None],
    )
    return (residual_g + entry_part, residual_round, query_g, own_g, vector_grads)


def partner(array, by):
    return lax.ppermute(array, "dp", [(i, i ^ by) for i in range(lax.axis_size("dp"))])


def gathered_rows(values, axis=0):
    return lax.all_gather(values, "seq", axis=axis, tiled=True)


def gathered_tokens(rows):
    line = gathered_rows(rows)
    both = jnp.concatenate([line, partner(line, 2)])
    return jnp.concatenate([both, partner(both, 1)])


def blocks_of(array, by, axis=1):
    index = lax.axis_index("dp")
    size = array.shape[axis] // lax.axis_size("dp")
    blocks = [
        lax.dynamic_slice_in_dim(array, (index ^ which) * size, size, axis) for which in by
    ]
    return blocks[0] if len(blocks) == 1 else jnp.concatenate(blocks, axis=axis)


def feed_forward_grads(all_normed_two, all_incoming, params):
    up_w, down_w, up_vec = params[2], params[3], params[6]
    share = up_w.shape[0] // lax.axis_size("dp")
    chip_columns = blocks_of(all_normed_two, (0, 1))
    own, sent = [], []
    for by in (0, 2):
        up_part, down_part = blocks_of(up_w, (by,)), blocks_of(down_w, (by,), 0)
        upper_act = jnp.dot(all_normed_two, up_part, preferred_element_type=jnp.float32)
        upper_act = upper_act + blocks_of(up_vec[None], (by,))
        hidden_f, gate_back = jax.vjp(smooth_gate, upper_act)
        hidden_g = jnp.einsum(
            "rd,fd->rf", all_incoming, down_part, preferred_element_type=jnp.float32
        )
        upper_round = gate_back(hidden_g)[0].astype(jnp.bfloat16)
        if by == 0:
            down_g = jnp.einsum(
                "rf,rd->fd",
                hidden_f.astype(jnp.bfloat16),
                all_incoming,
                preferred_element_type=jnp.float32,
            )
        up_g = jnp.einsum(
            "rd,rf->df", chip_columns, upper_round, preferred_element_type=jnp.float32
        )
        own.append(up_g[:share])
        sent.append(up_g[share:])
    received = partner(jnp.concatenate(sent, axis=1), 1)
    columns = own[0].shape[1]
    index = lax.axis_index("dp")
    total = jnp.zeros((share, up_w.shape[1]), jnp.float32)
    for by, part in (
        (0, own[0]),
        (2, own[1]),
        (1, received[:, :columns]),
        (3, received[:, columns:]),
    ):
        total = lax.dynamic_update_slice_in_dim(total, part, (index ^ by) * columns, 1)
    return (total, down_g)


def summed_product(left, right):
    line = gathered_rows(right)
    other = partner(line, 1)
    product = jnp.einsum("rd,re->de", left[0], line, preferred_element_type=jnp.float32)
    product = product + jnp.einsum(
        "rd,re->de", left[1], other, preferred_element_type=jnp.float32
    )
    share = product.shape[0] // 2
    received = partner(product[share:].astype(jnp.bfloat16), 2)
    return product[:share] + received.astype(jnp.float32)


def piece_plan(shapes):
    return [
        (which, part * (rows // (2 * pieces)), rows // (2 * pieces), rows // 2)
        for which, (rows, columns) in enumerate(shapes)
        for pieces in (2 if rows * columns > 512 * 1024 else 1,)
        for part in range(pieces)
    ]


def gather_kernel(plan, count, *refs):
    own, full = refs[:count], refs[count : 2 * count]
    (local_sem, own_send, own_recv, far_send, far_recv) = refs[2 * count : 2 * count + 5]
    (side_send, side_recv, near_send, near_recv, last_send, last_recv) = refs[2 * count + 5 :]
    me, place = lax.axis_index("dp"), lax.axis_index("seq")
    far = lax.rem(me + 2, 4)
    near = me + 1 - 2 * lax.rem(me, 2)
    half = lax.rem(place, 2)
    side = place + 1 - 2 * half
    barrier = pltpu.get_barrier_semaphore()
    for target in ({"dp": far}, {"dp": near}, {"seq": side}):
        pl.semaphore_signal(
            barrier, inc=1, device_id=target, device_id_type=pl.DeviceIdType.MESH
        )
    pl.semaphore_wait(barrier, 3)

    def rows_at(which_half, first, rows, half_rows):
        return pl.ds(pl.multiple_of(which_half * half_rows + first, rows), rows)

    def remote(source, target, send, recv, device):
        return pltpu.make_async_remote_copy(
            src_ref=source,
            dst_ref=target,
            send_sem=send,
            recv_sem=recv,
            device_id=device,
            device_id_type=pl.DeviceIdType.MESH,
        )

    far_copies, side_copies, near_copies, last_copies = [], [], [], []
    for index, (which, first, rows, half_rows) in enumerate(plan):
        span = rows_at(half, first, rows, half_rows)
        copy = remote(
            own[which].at[span],
            full[which].at[me, span],
            far_send.at[index],
            far_recv.at[index],
            {"dp": far},
        )
        copy.start()
        far_copies.append(copy)
    own_copies, local_copies = [], []
    for which in range(count):
        copy = remote(
            own[which], full[which].at[me], own_send.at[which], own_recv.at[which], {"dp": near}
        )
        copy.start()
        own_copies.append(copy)
        copy = pltpu.make_async_copy(own[which], full[which].at[me], local_sem.at[which])
        copy.start()
        local_copies.append(copy)

    def last_step(index):
        which, first, rows, half_rows = plan[index]
        side_copies[index].wait_recv()
        block = full[which].at[far, rows_at(1 - half, first, rows, half_rows)]
        copy = remote(block, block, last_send.at[index], last_recv.at[index], {"dp": near})
        copy.start()
        last_copies.append(copy)

    for index, (which, first, rows, half_rows) in enumerate(plan):
        far_copies[index].wait_recv()
        block = full[which].at[far, rows_at(half, first, rows, half_rows)]
        copy = remote(block, block, side_send.at[index], side_recv.at[index], {"seq": side})
        copy.start()
        side_copies.append(copy)
        copy = remote(block, block, near_send.at[index], near_recv.at[index], {"dp": near})
        copy.start()
        near_copies.append(copy)
        if index > 0:
            last_step(index - 1)
    last_step(len(plan) - 1)
    for copy in near_copies + last_copies + own_copies:
        copy.wait_recv()
    for copy in far_copies + side_copies + near_copies + last_copies + own_copies:
        copy.wait_send()
    for copy in local_copies:
        copy.wait()


def gathered_weights(weights):
    owners, places = lax.axis_size("dp"), lax.axis_size("seq")
    if owners != 4 or places % 2:
        return [lax.all_gather(weight, "dp", axis=0, tiled=True) for weight in weights]
    plan = piece_plan([weight.shape for weight in weights])
    count, pieces = len(weights), len(plan)
    dma = pltpu.SemaphoreType.DMA
    full = pl.pallas_call(
        lambda *refs: gather_kernel(plan, count, *refs),
        out_shape=[jax.ShapeDtypeStruct((owners,) + w.shape, w.dtype) for w in weights],
        in_specs=[pl.BlockSpec(memory_space=pltpu.VMEM)] * count,
        out_specs=[pl.BlockSpec(memory_space=pl.ANY)] * count,
        scratch_shapes=[dma((count,))] * 3 + [dma((pieces,))] * 8,
        compiler_params=pltpu.CompilerParams(collective_id=0, has_side_effects=True),
        name="gather_weights",
    )(*weights)
    return [whole.reshape(-1, whole.shape[2]) for whole in full]


def shards(
    ends_in, segments, qkv_weight, out_weight, up_weight, down_weight, gains, shifts, up_bias
):
    section_index = lax.axis_index("section")
    leading = section_index == 0
    outer, inner = lax.axis_size("dp"), lax.axis_size("seq")
    own_slot = ends_in[0]
    seq_count, tok_count, width = own_slot.shape
    share = width // outer
    packed = jnp.concatenate([gains[0].reshape(-1), shifts[0].reshape(-1), up_bias[0]])
    packed = lax.all_gather(packed, "dp", axis=0, tiled=False).astype(jnp.float32)
    gain_count, shift_count = gains.shape[1], shifts.shape[1]

    def rows_of(first, count):
        part = packed[:, first * share : (first + count) * share]
        return part.reshape(outer, count, share).transpose(1, 0, 2).reshape(count, width)

    params = (
        *gathered_weights((qkv_weight[0], out_weight[0], up_weight[0], down_weight[0])),
        rows_of(0, gain_count),
        rows_of(gain_count, shift_count),
        packed[:, (gain_count + shift_count) * share :].reshape(-1),
    )
    bias = score_bias(segments)

    first_output = forward(own_slot, params, bias)[0]
    received = passed_along(
        first_output.astype(jnp.bfloat16).reshape(own_slot.shape), "section", 1
    )
    entry_rows = jnp.where(leading, own_slot, received)
    last_output, saved = forward(entry_rows, params, bias)
    normed, query, own, halo, mixed, residual, normed_two, upper_act = saved
    all_normed_two = gathered_tokens(normed_two)
    mine = jnp.concatenate([blocks_of(normed, (0, 2)), blocks_of(mixed, (0, 2))], axis=1)
    theirs = jnp.concatenate([blocks_of(normed, (1, 3)), blocks_of(mixed, (1, 3))], axis=1)
    lefts = gathered_rows(jnp.stack([mine, partner(theirs, 1)]), 1)
    normed_left, mixed_left = lefts[:, :, : width // 2], lefts[:, :, width // 2 :]
    early_entry = backward(own_slot, entry_rows, params, saved, bias)[0]
    returned = passed_along(
        early_entry.astype(jnp.bfloat16).reshape(own_slot.shape), "section", -1
    )
    incoming = jnp.where(leading, returned, own_slot)
    all_incoming = gathered_tokens(incoming.reshape(-1, width))
    entry_g, residual_round, query_g, own_g, vector_grads = backward(
        incoming, entry_rows, params, saved, bias
    )
    out_total = summed_product(mixed_left, residual_round)
    qkv_total = jnp.concatenate(
        [
            summed_product(normed_left, part)
            for part in (query_g, own_g[:, :width], own_g[:, width:])
        ],
        axis=1,
    )
    up_total, down_total = feed_forward_grads(all_normed_two, all_incoming, params)
    vectors_g = jnp.concatenate([part.reshape(-1) for part in vector_grads])
    vectors_g = lax.psum(vectors_g, ("seq", "dp"))
    gain_size, shift_size = gain_count * width, shift_count * width
    gains_total = blocks_of(vectors_g[:gain_size].reshape(gain_count, width), (0,))
    shifts_total = vectors_g[gain_size : gain_size + shift_size].reshape(shift_count, width)
    shifts_total = blocks_of(shifts_total, (0,))
    up_bias_total = blocks_of(vectors_g[gain_size + shift_size :][None], (0,))[0]

    ends_out = jnp.where(leading, entry_g, last_output).reshape(own_slot.shape)[None]
    return (
        ends_out,
        qkv_total[None],
        out_total[None],
        up_total[None],
        down_total[None],
        gains_total[None],
        shifts_total[None],
        up_bias_total[None],
    )


def solution(mesh):
    in_specs = (
        P("section", "dp", "seq", None),
        P("dp", "seq"),
        P("section", "dp", None),
        P("section", "dp", None),
        P("section", "dp", None),
        P("section", "dp", None),
        P("section", None, "dp"),
        P("section", None, "dp"),
        P("section", "dp"),
    )
    out_specs = (
        P("section", "dp", "seq", None),
        P("section", "dp", None),
        P("section", "dp", None),
        P("section", "dp", None),
        P("section", "dp", None),
        P("section", None, "dp"),
        P("section", None, "dp"),
        P("section", "dp"),
    )
    return jax.shard_map(shards, mesh=mesh, in_specs=in_specs, out_specs=out_specs, check_vma=False)
```

```python
import jax
import jax.numpy as jnp
from jax import lax
from jax.experimental import pallas as pl
from jax.experimental.pallas import tpu as pltpu
from jax.sharding import PartitionSpec as P

DH = 64


EPSILON = 1e-05
MASKED = -1e30


def passed_along(array, axis, by):
    count = lax.axis_size(axis)
    pairs = [(i, i + by) for i in range(count) if 0 <= i + by < count]
    return lax.ppermute(array, axis, pairs)


def layer_norm(row_values, gain_vec, shift_vec):
    center = row_values - jnp.mean(row_values, axis=-1, keepdims=True)
    spread = jnp.mean(center * center, axis=-1, keepdims=True)
    return center * lax.rsqrt(spread + EPSILON) * gain_vec + shift_vec


def smooth_gate(upper_act):
    return jax.nn.gelu(upper_act, approximate=True)


def halo_chunks():
    return max(1, lax.axis_size("seq") // 4)


def from_before(array):
    return jnp.stack([passed_along(array, "seq", by) for by in range(halo_chunks(), 0, -1)])


def score_bias(segments):
    chunks = halo_chunks()
    tok_count = segments.shape[1]
    place = lax.axis_index("seq")
    before = from_before(segments)
    window = [
        jnp.where(place >= chunks - chunk, before[chunk], -1) for chunk in range(chunks)
    ] + [segments]
    keys = jnp.concatenate(window, axis=1)
    query_pos = lax.iota(jnp.int32, tok_count) + chunks * tok_count
    key_pos = lax.iota(jnp.int32, keys.shape[1])
    allowed = (key_pos[None, :] <= query_pos[:, None])[None]
    allowed = allowed & (keys[:, None, :] == segments[:, :, None])
    return jnp.where(allowed, 0.0, MASKED).astype(jnp.float32)


def halves_of(pair):
    lane = lax.broadcasted_iota(jnp.int32, pair.shape, 1)
    low = jnp.where(lane < DH, pair, jnp.zeros_like(pair))
    high = jnp.where(lane < DH, jnp.zeros_like(pair), pair)
    return jnp.concatenate([low, high], axis=0)


def joined_halves(stacked):
    tok_count = stacked.shape[0] // 2
    low, high = stacked[:tok_count], stacked[tok_count:]
    return jnp.where(lax.broadcasted_iota(jnp.int32, low.shape, 1) < DH, low, high)


def dot_last(left, right):
    return lax.dot_general(
        left, right, (((1,), (1,)), ((), ())), preferred_element_type=jnp.float32
    )


def dot_first(left, right):
    return lax.dot_general(
        left, right, (((0,), (0,)), ((), ())), preferred_element_type=jnp.float32
    )


def pair_scores(query_pair, key_pair, bias):
    scores = dot_last(halves_of(query_pair), key_pair) * DH ** (-0.5)
    scores = scores + jnp.concatenate([bias, bias], axis=0)
    row_max = jnp.max(scores, axis=-1, keepdims=True)
    log_total = jnp.log(jnp.sum(jnp.exp(scores - row_max), axis=-1, keepdims=True)) + row_max
    return jnp.exp(scores - log_total)


def window_pair(halo_ref, own_ref, rows, first):
    columns = pl.ds(first, 2 * DH)
    parts = [halo_ref[chunk, rows, columns] for chunk in range(halo_ref.shape[0])]
    return jnp.concatenate(parts + [own_ref[rows, columns]], axis=0)


def attend_kernel(query_ref, own_ref, halo_ref, bias_ref, out_ref):
    tok_count, width = bias_ref.shape[1], query_ref.shape[1]
    for sequence in range(bias_ref.shape[0]):
        rows = pl.ds(sequence * tok_count, tok_count)
        bias = bias_ref[sequence]
        for first in range(0, width, 2 * DH):
            weights = pair_scores(
                query_ref[rows, pl.ds(first, 2 * DH)],
                window_pair(halo_ref, own_ref, rows, first),
                bias,
            )
            values = window_pair(halo_ref, own_ref, rows, width + first)
            attended = jnp.dot(
                weights.astype(jnp.bfloat16), values, preferred_element_type=jnp.float32
            )
            out_ref[rows, pl.ds(first, 2 * DH)] = joined_halves(attended).astype(jnp.bfloat16)


def attend_grad_kernel(
    query_ref, own_ref, halo_ref, bias_ref, out_ref, grad_ref, query_g_ref, own_g_ref, halo_g_ref
):
    tok_count, width = bias_ref.shape[1], query_ref.shape[1]
    chunks = halo_ref.shape[0]
    for sequence in range(bias_ref.shape[0]):
        rows = pl.ds(sequence * tok_count, tok_count)
        bias = bias_ref[sequence]
        for first in range(0, width, 2 * DH):
            columns = pl.ds(first, 2 * DH)
            query_pair, grad_pair = query_ref[rows, columns], grad_ref[rows, columns]
            keys = window_pair(halo_ref, own_ref, rows, first)
            values = window_pair(halo_ref, own_ref, rows, width + first)
            weights = pair_scores(query_pair, keys, bias)
            queries_two, grads_two = halves_of(query_pair), halves_of(grad_pair)
            products = grads_two.astype(jnp.float32) * halves_of(out_ref[rows, columns]).astype(
                jnp.float32
            )
            row_delta = jnp.sum(products, axis=-1, keepdims=True)
            scores_g = (weights * (dot_last(grads_two, values) - row_delta)).astype(jnp.bfloat16)
            query_g = jnp.dot(scores_g, keys, preferred_element_type=jnp.float32)
            query_g_ref[rows, columns] = (joined_halves(query_g) * DH ** (-0.5)).astype(
                jnp.bfloat16
            )
            keys_g = dot_first(scores_g, queries_two) * DH ** (-0.5)
            values_g = dot_first(weights.astype(jnp.bfloat16), grads_two)
            for grad, start in ((keys_g, first), (values_g, width + first)):
                for chunk in range(chunks):
                    halo_g_ref[chunk, rows, pl.ds(start, 2 * DH)] = grad[
                        chunk * tok_count : (chunk + 1) * tok_count
                    ].astype(jnp.bfloat16)
                own_g_ref[rows, pl.ds(start, 2 * DH)] = grad[chunks * tok_count :]


def in_vmem(count):
    return [pl.BlockSpec(memory_space=pltpu.VMEM)] * count


def attend(query, own, halo, bias):
    return pl.pallas_call(
        attend_kernel,
        out_shape=jax.ShapeDtypeStruct(query.shape, jnp.bfloat16),
        in_specs=in_vmem(4),
        out_specs=pl.BlockSpec(memory_space=pltpu.VMEM),
        cost_estimate=pl.CostEstimate(flops=10**9, bytes_accessed=10**7, transcendentals=0),
        name="attend",
    )(query, own, halo, bias)


def attend_grad(query, own, halo, bias, attended, heads_grad):
    return pl.pallas_call(
        attend_grad_kernel,
        out_shape=(
            jax.ShapeDtypeStruct(query.shape, jnp.bfloat16),
            jax.ShapeDtypeStruct(own.shape, jnp.float32),
            jax.ShapeDtypeStruct(halo.shape, jnp.bfloat16),
        ),
        in_specs=in_vmem(6),
        out_specs=tuple(in_vmem(3)),
        cost_estimate=pl.CostEstimate(flops=10**9, bytes_accessed=10**7, transcendentals=0),
        name="attend_grad",
    )(query, own, halo, bias, attended, heads_grad)


def forward(entry_rows, params, bias):
    qkv_w, out_w, up_w, down_w, gain_vecs, vectors, up_vec = params
    width = entry_rows.shape[-1]
    row_values = entry_rows.reshape(-1, width).astype(jnp.float32)
    normed = layer_norm(row_values, gain_vecs[0], vectors[0]).astype(jnp.bfloat16)
    own_bias = jnp.concatenate([jnp.zeros_like(vectors[2]), vectors[2]])
    own = jnp.dot(normed, qkv_w[:, width:], preferred_element_type=jnp.float32) + own_bias
    own = own.astype(jnp.bfloat16)
    halo = from_before(own)
    query = jnp.dot(normed, qkv_w[:, :width], preferred_element_type=jnp.float32) + vectors[1]
    query = query.astype(jnp.bfloat16)
    mixed = attend(query, own, halo, bias)
    residual = row_values + jnp.dot(mixed, out_w, preferred_element_type=jnp.float32) + vectors[3]
    normed_two = layer_norm(residual, gain_vecs[1], vectors[4]).astype(jnp.bfloat16)
    upper_act = jnp.dot(normed_two, up_w, preferred_element_type=jnp.float32) + up_vec
    hidden = smooth_gate(upper_act).astype(jnp.bfloat16)
    output = residual + jnp.dot(hidden, down_w, preferred_element_type=jnp.float32) + vectors[5]
    return (output, (normed, query, own, halo, mixed, residual, normed_two, upper_act))


def backward(incoming, entry_rows, params, saved, bias):
    qkv_w, out_w, up_w, down_w, gain_vecs, vectors, up_vec = params
    normed, query, own, halo, mixed, residual, normed_two, upper_act = saved
    width = entry_rows.shape[-1]
    grad_rows = incoming.reshape(-1, width)
    upstream = grad_rows.astype(jnp.float32)
    down_bias_g = jnp.sum(upstream, axis=0)
    hidden_g = jnp.einsum("rd,fd->rf", grad_rows, down_w, preferred_element_type=jnp.float32)
    upper_g = jax.vjp(smooth_gate, upper_act)[1](hidden_g)[0]
    up_bias_g = jnp.sum(upper_g, axis=0)
    normed_two_g = jnp.einsum(
        "rf,df->rd", upper_g.astype(jnp.bfloat16), up_w, preferred_element_type=jnp.float32
    )
    norm_back = jax.vjp(layer_norm, residual, gain_vecs[1], vectors[4])[1]
    residual_part, gain_two_g, shift_two_g = norm_back(normed_two_g)
    residual_g = upstream + residual_part
    residual_round = residual_g.astype(jnp.bfloat16)
    out_bias_g = jnp.sum(residual_g, axis=0)
    mixed_g = jnp.einsum(
        "re,de->rd", residual_round, out_w, preferred_element_type=jnp.float32
    ).astype(jnp.bfloat16)
    query_g, own_g, halo_g = attend_grad(query, own, halo, bias, mixed, mixed_g)
    chunks = halo_g.shape[0]
    for chunk in range(chunks):
        own_g = own_g + passed_along(halo_g[chunk], "seq", chunk - chunks).astype(jnp.float32)
    own_g = own_g.astype(jnp.bfloat16)
    column_sums = jnp.sum(query_g.astype(jnp.float32), axis=0)
    value_sums = jnp.sum(own_g[:, width:].astype(jnp.float32), axis=0)
    normed_g = jnp.einsum(
        "re,de->rd", query_g, qkv_w[:, :width], preferred_element_type=jnp.float32
    ) + jnp.einsum("re,de->rd", own_g, qkv_w[:, width:], preferred_element_type=jnp.float32)
    row_values = entry_rows.reshape(-1, width).astype(jnp.float32)
    entry_back = jax.vjp(layer_norm, row_values, gain_vecs[0], vectors[0])[1]
    entry_part, gain_one_g, shift_one_g = entry_back(normed_g)
    vector_grads = (
        jnp.stack([gain_one_g, gain_two_g]),
        jnp.stack(
            [shift_one_g, column_sums, value_sums, out_bias_g, shift_two_g, down_bias_g]
        ),
        up_bias_g[None],
    )
    return (residual_g + entry_part, residual_round, query_g, own_g, vector_grads)


def partner(array, by):
    return lax.ppermute(array, "dp", [(i, i ^ by) for i in range(lax.axis_size("dp"))])


def gathered_rows(values, axis=0):
    return lax.all_gather(values, "seq", axis=axis, tiled=True)


def gathered_tokens(line):
    both = jnp.concatenate([line, partner(line, 2)])
    return jnp.concatenate([both, partner(both, 1)])


def blocks_of(array, by, axis=1):
    index = lax.axis_index("dp")
    size = array.shape[axis] // lax.axis_size("dp")
    blocks = [
        lax.dynamic_slice_in_dim(array, (index ^ which) * size, size, axis) for which in by
    ]
    return blocks[0] if len(blocks) == 1 else jnp.concatenate(blocks, axis=axis)


def feed_forward_block(all_normed_two, all_incoming, params, by):
    up_w, down_w, up_vec = params[2], params[3], params[6]
    up_part, down_part = blocks_of(up_w, (by,)), blocks_of(down_w, (by,), 0)
    upper_act = jnp.dot(all_normed_two, up_part, preferred_element_type=jnp.float32)
    upper_act = upper_act + blocks_of(up_vec[None], (by,))
    hidden_f, gate_back = jax.vjp(smooth_gate, upper_act)
    hidden_g = jnp.einsum("rd,fd->rf", all_incoming, down_part, preferred_element_type=jnp.float32)
    upper_round = lax.optimization_barrier(gate_back(hidden_g)[0].astype(jnp.bfloat16))
    chip_columns = blocks_of(all_normed_two, (0, 1))
    up_g = jnp.einsum("rd,rf->df", chip_columns, upper_round, preferred_element_type=jnp.float32)
    if by:
        return up_g
    hidden = hidden_f.astype(jnp.bfloat16)
    down_g = jnp.einsum("rf,rd->fd", hidden, all_incoming, preferred_element_type=jnp.float32)
    return (up_g, down_g)


def up_blocks(own_first, own_second, received, share):
    columns = own_first.shape[1]
    index, count = lax.axis_index("dp"), lax.axis_size("dp")
    total = jnp.zeros((share, count * columns), jnp.float32)
    for by, part in (
        (0, own_first[:share]),
        (2, own_second[:share]),
        (1, received[:, :columns]),
        (3, received[:, columns:]),
    ):
        total = lax.dynamic_update_slice_in_dim(total, part, (index ^ by) * columns, 1)
    return total


def product(left, line, other):
    total = jnp.einsum("rd,re->de", left[0], line, preferred_element_type=jnp.float32)
    return total + jnp.einsum("rd,re->de", left[1], other, preferred_element_type=jnp.float32)


def summed_shares(vector):
    for by in (1, 2):
        vector = vector + partner(vector, by)
    by, count = 1, lax.axis_size("seq")
    while by < count:
        vector = vector + lax.ppermute(vector, "seq", [(i, i ^ by) for i in range(count)])
        by *= 2
    return vector


def by_owner(array, owners):
    rows, columns = array.shape
    return array.reshape(rows, owners, -1).transpose(1, 0, 2).reshape(owners, -1)


def piece_plan(shapes):
    return [
        (which, part * (rows // (2 * pieces)), rows // (2 * pieces), rows // 2)
        for which, (rows, columns) in enumerate(shapes)
        for pieces in (2 if rows * columns > 512 * 1024 else 1,)
        for part in range(pieces)
    ]


def gather_kernel(plan, count, *refs):
    own, full = refs[:count], refs[count : 2 * count]
    (local_sem, own_send, own_recv, far_send, far_recv) = refs[2 * count : 2 * count + 5]
    (side_send, side_recv, near_send, near_recv, last_send, last_recv) = refs[2 * count + 5 :]
    me, place = lax.axis_index("dp"), lax.axis_index("seq")
    far = lax.rem(me + 2, 4)
    near = me + 1 - 2 * lax.rem(me, 2)
    half = lax.rem(place, 2)
    side = place + 1 - 2 * half
    barrier = pltpu.get_barrier_semaphore()
    for target in ({"dp": far}, {"dp": near}, {"seq": side}):
        pl.semaphore_signal(
            barrier, inc=1, device_id=target, device_id_type=pl.DeviceIdType.MESH
        )
    pl.semaphore_wait(barrier, 3)

    def rows_at(which_half, first, rows, half_rows):
        return pl.ds(pl.multiple_of(which_half * half_rows + first, rows), rows)

    def remote(source, target, send, recv, device):
        return pltpu.make_async_remote_copy(
            src_ref=source,
            dst_ref=target,
            send_sem=send,
            recv_sem=recv,
            device_id=device,
            device_id_type=pl.DeviceIdType.MESH,
        )

    far_copies, side_copies, near_copies, last_copies = [], [], [], []
    for index, (which, first, rows, half_rows) in enumerate(plan):
        span = rows_at(half, first, rows, half_rows)
        copy = remote(
            own[which].at[span],
            full[which].at[me, span],
            far_send.at[index],
            far_recv.at[index],
            {"dp": far},
        )
        copy.start()
        far_copies.append(copy)
    own_copies, local_copies = [], []
    for which in range(count):
        copy = remote(
            own[which], full[which].at[me], own_send.at[which], own_recv.at[which], {"dp": near}
        )
        copy.start()
        own_copies.append(copy)
        copy = pltpu.make_async_copy(own[which], full[which].at[me], local_sem.at[which])
        copy.start()
        local_copies.append(copy)

    def last_step(index):
        which, first, rows, half_rows = plan[index]
        side_copies[index].wait_recv()
        block = full[which].at[far, rows_at(1 - half, first, rows, half_rows)]
        copy = remote(block, block, last_send.at[index], last_recv.at[index], {"dp": near})
        copy.start()
        last_copies.append(copy)

    for index, (which, first, rows, half_rows) in enumerate(plan):
        far_copies[index].wait_recv()
        block = full[which].at[far, rows_at(half, first, rows, half_rows)]
        copy = remote(block, block, side_send.at[index], side_recv.at[index], {"seq": side})
        copy.start()
        side_copies.append(copy)
        copy = remote(block, block, near_send.at[index], near_recv.at[index], {"dp": near})
        copy.start()
        near_copies.append(copy)
        if index > 0:
            last_step(index - 1)
    last_step(len(plan) - 1)
    for copy in near_copies + last_copies + own_copies:
        copy.wait_recv()
    for copy in far_copies + side_copies + near_copies + last_copies + own_copies:
        copy.wait_send()
    for copy in local_copies:
        copy.wait()


def gathered_weights(weights):
    owners, places = lax.axis_size("dp"), lax.axis_size("seq")
    if owners != 4 or places % 2:
        return [lax.all_gather(weight, "dp", axis=0, tiled=True) for weight in weights]
    plan = piece_plan([weight.shape for weight in weights])
    count, pieces = len(weights), len(plan)
    dma = pltpu.SemaphoreType.DMA
    full = pl.pallas_call(
        lambda *refs: gather_kernel(plan, count, *refs),
        out_shape=[jax.ShapeDtypeStruct((owners,) + w.shape, w.dtype) for w in weights],
        in_specs=[pl.BlockSpec(memory_space=pltpu.VMEM)] * count,
        out_specs=[pl.BlockSpec(memory_space=pl.ANY)] * count,
        scratch_shapes=[dma((count,))] * 3 + [dma((pieces,))] * 8,
        compiler_params=pltpu.CompilerParams(collective_id=0, has_side_effects=True),
        name="gather_weights",
    )(*weights)
    return [whole.reshape(-1, whole.shape[2]) for whole in full]


def shards(
    ends_in, segments, qkv_weight, out_weight, up_weight, down_weight, gains, shifts, up_bias
):
    section_index = lax.axis_index("section")
    leading = section_index == 0
    outer, inner = lax.axis_size("dp"), lax.axis_size("seq")
    own_slot = ends_in[0]
    seq_count, tok_count, width = own_slot.shape
    share = width // outer
    packed = jnp.concatenate([gains[0].reshape(-1), shifts[0].reshape(-1), up_bias[0]])
    packed = lax.all_gather(packed, "dp", axis=0, tiled=False).astype(jnp.float32)
    gain_count, shift_count = gains.shape[1], shifts.shape[1]

    def rows_of(first, count):
        part = packed[:, first * share : (first + count) * share]
        return part.reshape(outer, count, share).transpose(1, 0, 2).reshape(count, width)

    params = (
        *gathered_weights((qkv_weight[0], out_weight[0], up_weight[0], down_weight[0])),
        rows_of(0, gain_count),
        rows_of(gain_count, shift_count),
        packed[:, (gain_count + shift_count) * share :].reshape(-1),
    )
    bias = score_bias(segments)

    first_output = forward(own_slot, params, bias)[0]
    received = passed_along(
        first_output.astype(jnp.bfloat16).reshape(own_slot.shape), "section", 1
    )
    entry_rows = jnp.where(leading, own_slot, received)
    last_output, saved = forward(entry_rows, params, bias)
    normed, query, own, halo, mixed, residual, normed_two, upper_act = saved
    normed_two_line = gathered_rows(normed_two)
    mine = jnp.concatenate([blocks_of(normed, (0, 2)), blocks_of(mixed, (0, 2))], axis=1)
    theirs = jnp.concatenate([blocks_of(normed, (1, 3)), blocks_of(mixed, (1, 3))], axis=1)
    lefts = gathered_rows(jnp.stack([mine, partner(theirs, 1)]), 1)
    early_entry = backward(own_slot, entry_rows, params, saved, bias)[0]
    returned = passed_along(
        early_entry.astype(jnp.bfloat16).reshape(own_slot.shape), "section", -1
    )
    incoming = jnp.where(leading, returned, own_slot)
    incoming_rows, normed_two_line, lefts = lax.optimization_barrier(
        (incoming.reshape(-1, width), normed_two_line, lefts)
    )
    normed_left, mixed_left = lefts[:, :, : width // 2], lefts[:, :, width // 2 :]
    incoming_line = gathered_rows(incoming_rows)
    entry_g, residual_round, query_g, own_g, vector_grads = backward(
        incoming, entry_rows, params, saved, bias
    )
    first_line = gathered_rows(jnp.concatenate([residual_round, query_g], axis=1))
    second_line = gathered_rows(own_g)
    all_normed_two = gathered_tokens(normed_two_line)
    all_incoming = gathered_tokens(incoming_line)
    up_first, down_total = feed_forward_block(all_normed_two, all_incoming, params, 0)
    up_first, down_total, first_line = lax.optimization_barrier((up_first, down_total, first_line))
    first_other = partner(first_line, 1)
    up_second = feed_forward_block(all_normed_two, all_incoming, params, 2)
    up_sent = partner(jnp.concatenate([up_first[share:], up_second[share:]], axis=1), 1)
    out_g = product(mixed_left, first_line[:, :width], first_other[:, :width])
    query_wg = product(normed_left, first_line[:, width:], first_other[:, width:])
    first_sent = jnp.concatenate([out_g[share:], query_wg[share:]], axis=1).astype(jnp.bfloat16)
    first_sent = partner(first_sent, 2)
    up_second, second_line = lax.optimization_barrier((up_second, second_line))
    second_other = partner(second_line, 1)
    own_wg = product(normed_left, second_line, second_other)
    second_sent = partner(own_wg[share:].astype(jnp.bfloat16), 2)
    out_total = out_g[:share] + first_sent[:, :width].astype(jnp.float32)
    qkv_total = jnp.concatenate(
        [
            query_wg[:share] + first_sent[:, width:].astype(jnp.float32),
            own_wg[:share] + second_sent.astype(jnp.float32),
        ],
        axis=1,
    )
    up_total = up_blocks(up_first, up_second, up_sent, share)
    vectors_g = jnp.concatenate([by_owner(part, outer) for part in vector_grads], axis=1)
    summed = summed_shares(vectors_g.reshape(-1, 128)).reshape(outer, -1)
    own_vectors = lax.dynamic_index_in_dim(summed, lax.axis_index("dp"), 0, keepdims=False)
    gains_total = own_vectors[: gain_count * share].reshape(gain_count, share)
    shifts_total = own_vectors[gain_count * share : (gain_count + shift_count) * share]
    shifts_total = shifts_total.reshape(shift_count, share)
    up_bias_total = own_vectors[(gain_count + shift_count) * share :]

    ends_out = jnp.where(leading, entry_g, last_output).reshape(own_slot.shape)[None]
    return (
        ends_out,
        qkv_total[None],
        out_total[None],
        up_total[None],
        down_total[None],
        gains_total[None],
        shifts_total[None],
        up_bias_total[None],
    )


def solution(mesh):
    in_specs = (
        P("section", "dp", "seq", None),
        P("dp", "seq"),
        P("section", "dp", None),
        P("section", "dp", None),
        P("section", "dp", None),
        P("section", "dp", None),
        P("section", None, "dp"),
        P("section", None, "dp"),
        P("section", "dp"),
    )
    out_specs = (
        P("section", "dp", "seq", None),
        P("section", "dp", None),
        P("section", "dp", None),
        P("section", "dp", None),
        P("section", "dp", None),
        P("section", None, "dp"),
        P("section", None, "dp"),
        P("section", "dp"),
    )
    return jax.shard_map(shards, mesh=mesh, in_specs=in_specs, out_specs=out_specs, check_vma=False)
```

```python
import jax
import jax.numpy as jnp
from jax import lax
from jax.experimental import pallas as pl
from jax.experimental.pallas import tpu as pltpu
from jax.sharding import PartitionSpec as P

DH = 64


EPSILON = 1e-05
MASKED = -1e30


def passed_along(array, axis, by):
    count = lax.axis_size(axis)
    pairs = [(i, i + by) for i in range(count) if 0 <= i + by < count]
    return lax.ppermute(array, axis, pairs)


def layer_norm(row_values, gain_vec, shift_vec):
    center = row_values - jnp.mean(row_values, axis=-1, keepdims=True)
    spread = jnp.mean(center * center, axis=-1, keepdims=True)
    return center * lax.rsqrt(spread + EPSILON) * gain_vec + shift_vec


def smooth_gate(upper_act):
    return jax.nn.gelu(upper_act, approximate=True)


def halo_chunks():
    return max(1, lax.axis_size("seq") // 4)


def from_before(array):
    return jnp.stack([passed_along(array, "seq", by) for by in range(halo_chunks(), 0, -1)])


def score_bias(segments):
    chunks = halo_chunks()
    tok_count = segments.shape[1]
    place = lax.axis_index("seq")
    before = from_before(segments)
    window = [
        jnp.where(place >= chunks - chunk, before[chunk], -1) for chunk in range(chunks)
    ] + [segments]
    keys = jnp.concatenate(window, axis=1)
    query_pos = lax.iota(jnp.int32, tok_count) + chunks * tok_count
    key_pos = lax.iota(jnp.int32, keys.shape[1])
    allowed = (key_pos[None, :] <= query_pos[:, None])[None]
    allowed = allowed & (keys[:, None, :] == segments[:, :, None])
    return jnp.where(allowed, 0.0, MASKED).astype(jnp.float32)


def halves_of(pair):
    lane = lax.broadcasted_iota(jnp.int32, pair.shape, 1)
    low = jnp.where(lane < DH, pair, jnp.zeros_like(pair))
    high = jnp.where(lane < DH, jnp.zeros_like(pair), pair)
    return jnp.concatenate([low, high], axis=0)


def joined_halves(stacked):
    tok_count = stacked.shape[0] // 2
    low, high = stacked[:tok_count], stacked[tok_count:]
    return jnp.where(lax.broadcasted_iota(jnp.int32, low.shape, 1) < DH, low, high)


def dot_last(left, right):
    return lax.dot_general(
        left, right, (((1,), (1,)), ((), ())), preferred_element_type=jnp.float32
    )


def dot_first(left, right):
    return lax.dot_general(
        left, right, (((0,), (0,)), ((), ())), preferred_element_type=jnp.float32
    )


def pair_scores(query_pair, key_pair, bias):
    scores = dot_last(halves_of(query_pair), key_pair) * DH ** (-0.5)
    scores = scores + jnp.concatenate([bias, bias], axis=0)
    row_max = jnp.max(scores, axis=-1, keepdims=True)
    log_total = jnp.log(jnp.sum(jnp.exp(scores - row_max), axis=-1, keepdims=True)) + row_max
    return jnp.exp(scores - log_total)


def window_pair(halo_ref, own_ref, rows, first):
    columns = pl.ds(first, 2 * DH)
    parts = [halo_ref[chunk, rows, columns] for chunk in range(halo_ref.shape[0])]
    return jnp.concatenate(parts + [own_ref[rows, columns]], axis=0)


def attend_kernel(query_ref, own_ref, halo_ref, bias_ref, out_ref):
    tok_count, width = bias_ref.shape[1], query_ref.shape[1]
    for sequence in range(bias_ref.shape[0]):
        rows = pl.ds(sequence * tok_count, tok_count)
        bias = bias_ref[sequence]
        for first in range(0, width, 2 * DH):
            weights = pair_scores(
                query_ref[rows, pl.ds(first, 2 * DH)],
                window_pair(halo_ref, own_ref, rows, first),
                bias,
            )
            values = window_pair(halo_ref, own_ref, rows, width + first)
            attended = jnp.dot(
                weights.astype(jnp.bfloat16), values, preferred_element_type=jnp.float32
            )
            out_ref[rows, pl.ds(first, 2 * DH)] = joined_halves(attended).astype(jnp.bfloat16)


def attend_grad_kernel(
    query_ref, own_ref, halo_ref, bias_ref, out_ref, grad_ref, query_g_ref, own_g_ref, halo_g_ref
):
    tok_count, width = bias_ref.shape[1], query_ref.shape[1]
    chunks = halo_ref.shape[0]
    for sequence in range(bias_ref.shape[0]):
        rows = pl.ds(sequence * tok_count, tok_count)
        bias = bias_ref[sequence]
        for first in range(0, width, 2 * DH):
            columns = pl.ds(first, 2 * DH)
            query_pair, grad_pair = query_ref[rows, columns], grad_ref[rows, columns]
            keys = window_pair(halo_ref, own_ref, rows, first)
            values = window_pair(halo_ref, own_ref, rows, width + first)
            weights = pair_scores(query_pair, keys, bias)
            queries_two, grads_two = halves_of(query_pair), halves_of(grad_pair)
            products = grads_two.astype(jnp.float32) * halves_of(out_ref[rows, columns]).astype(
                jnp.float32
            )
            row_delta = jnp.sum(products, axis=-1, keepdims=True)
            scores_g = (weights * (dot_last(grads_two, values) - row_delta)).astype(jnp.bfloat16)
            query_g = jnp.dot(scores_g, keys, preferred_element_type=jnp.float32)
            query_g_ref[rows, columns] = (joined_halves(query_g) * DH ** (-0.5)).astype(
                jnp.bfloat16
            )
            keys_g = dot_first(scores_g, queries_two) * DH ** (-0.5)
            values_g = dot_first(weights.astype(jnp.bfloat16), grads_two)
            for grad, start in ((keys_g, first), (values_g, width + first)):
                for chunk in range(chunks):
                    halo_g_ref[chunk, rows, pl.ds(start, 2 * DH)] = grad[
                        chunk * tok_count : (chunk + 1) * tok_count
                    ].astype(jnp.bfloat16)
                own_g_ref[rows, pl.ds(start, 2 * DH)] = grad[chunks * tok_count :]


def in_vmem(count):
    return [pl.BlockSpec(memory_space=pltpu.VMEM)] * count


def attend(query, own, halo, bias):
    return pl.pallas_call(
        attend_kernel,
        out_shape=jax.ShapeDtypeStruct(query.shape, jnp.bfloat16),
        in_specs=in_vmem(4),
        out_specs=pl.BlockSpec(memory_space=pltpu.VMEM),
        cost_estimate=pl.CostEstimate(flops=10**9, bytes_accessed=10**7, transcendentals=0),
        name="attend",
    )(query, own, halo, bias)


def attend_grad(query, own, halo, bias, attended, heads_grad):
    return pl.pallas_call(
        attend_grad_kernel,
        out_shape=(
            jax.ShapeDtypeStruct(query.shape, jnp.bfloat16),
            jax.ShapeDtypeStruct(own.shape, jnp.float32),
            jax.ShapeDtypeStruct(halo.shape, jnp.bfloat16),
        ),
        in_specs=in_vmem(6),
        out_specs=tuple(in_vmem(3)),
        cost_estimate=pl.CostEstimate(flops=10**9, bytes_accessed=10**7, transcendentals=0),
        name="attend_grad",
    )(query, own, halo, bias, attended, heads_grad)


def forward(entry_rows, params, bias):
    qkv_w, out_w, up_w, down_w, gain_vecs, vectors, up_vec = params
    width = entry_rows.shape[-1]
    row_values = entry_rows.reshape(-1, width).astype(jnp.float32)
    normed = layer_norm(row_values, gain_vecs[0], vectors[0]).astype(jnp.bfloat16)
    own_bias = jnp.concatenate([jnp.zeros_like(vectors[2]), vectors[2]])
    own = jnp.dot(normed, qkv_w[:, width:], preferred_element_type=jnp.float32) + own_bias
    own = own.astype(jnp.bfloat16)
    halo = from_before(own)
    normed_pair = own_left(normed)
    halo, normed_pair = lax.optimization_barrier((halo, normed_pair))
    query = jnp.dot(normed, qkv_w[:, :width], preferred_element_type=jnp.float32) + vectors[1]
    query = query.astype(jnp.bfloat16)
    mixed = attend(query, own, halo, bias)
    residual = row_values + jnp.dot(mixed, out_w, preferred_element_type=jnp.float32) + vectors[3]
    normed_two = layer_norm(residual, gain_vecs[1], vectors[4]).astype(jnp.bfloat16)
    upper_act = jnp.dot(normed_two, up_w, preferred_element_type=jnp.float32) + up_vec
    hidden = smooth_gate(upper_act).astype(jnp.bfloat16)
    output = residual + jnp.dot(hidden, down_w, preferred_element_type=jnp.float32) + vectors[5]
    saved = (normed_pair, query, own, halo, mixed, residual, normed_two, upper_act)
    return (output, saved)


def backward(incoming, entry_rows, params, saved, bias, beside=None):
    qkv_w, out_w, up_w, down_w, gain_vecs, vectors, up_vec = params
    normed_pair, query, own, halo, mixed, residual, normed_two, upper_act = saved
    width = entry_rows.shape[-1]
    grad_rows = incoming.reshape(-1, width)
    upstream = grad_rows.astype(jnp.float32)
    down_bias_g = jnp.sum(upstream, axis=0)
    hidden_g = jnp.einsum("rd,fd->rf", grad_rows, down_w, preferred_element_type=jnp.float32)
    upper_g = jax.vjp(smooth_gate, upper_act)[1](hidden_g)[0]
    up_bias_g = jnp.sum(upper_g, axis=0)
    normed_two_g = jnp.einsum(
        "rf,df->rd", upper_g.astype(jnp.bfloat16), up_w, preferred_element_type=jnp.float32
    )
    norm_back = jax.vjp(layer_norm, residual, gain_vecs[1], vectors[4])[1]
    residual_part, gain_two_g, shift_two_g = norm_back(normed_two_g)
    residual_g = upstream + residual_part
    residual_round = residual_g.astype(jnp.bfloat16)
    out_bias_g = jnp.sum(residual_g, axis=0)
    mixed_g = jnp.einsum(
        "re,de->rd", residual_round, out_w, preferred_element_type=jnp.float32
    ).astype(jnp.bfloat16)
    query_g, own_g, halo_g = attend_grad(query, own, halo, bias, mixed, mixed_g)
    if beside is not None:
        query_g, halo_g, beside = lax.optimization_barrier((query_g, halo_g, beside))
    chunks = halo_g.shape[0]
    for chunk in range(chunks):
        own_g = own_g + passed_along(halo_g[chunk], "seq", chunk - chunks).astype(jnp.float32)
    own_g = own_g.astype(jnp.bfloat16)
    column_sums = jnp.sum(query_g.astype(jnp.float32), axis=0)
    value_sums = jnp.sum(own_g[:, width:].astype(jnp.float32), axis=0)
    normed_g = jnp.einsum(
        "re,de->rd", query_g, qkv_w[:, :width], preferred_element_type=jnp.float32
    ) + jnp.einsum("re,de->rd", own_g, qkv_w[:, width:], preferred_element_type=jnp.float32)
    row_values = entry_rows.reshape(-1, width).astype(jnp.float32)
    entry_back = jax.vjp(layer_norm, row_values, gain_vecs[0], vectors[0])[1]
    entry_part, gain_one_g, shift_one_g = entry_back(normed_g)
    vector_grads = (
        jnp.stack([gain_one_g, gain_two_g]),
        jnp.stack(
            [shift_one_g, column_sums, value_sums, out_bias_g, shift_two_g, down_bias_g]
        ),
        up_bias_g[None],
    )
    return (residual_g + entry_part, residual_round, query_g, own_g, vector_grads, beside)


def partner(array, by):
    return lax.ppermute(array, "dp", [(i, i ^ by) for i in range(lax.axis_size("dp"))])


def gathered_rows(values, axis=0):
    return lax.all_gather(values, "seq", axis=axis, tiled=True)


def gathered_tokens(line):
    both = jnp.concatenate([line, partner(line, 2)])
    return jnp.concatenate([both, partner(both, 1)])


def blocks_of(array, by, axis=1):
    index = lax.axis_index("dp")
    size = array.shape[axis] // lax.axis_size("dp")
    blocks = [
        lax.dynamic_slice_in_dim(array, (index ^ which) * size, size, axis) for which in by
    ]
    return blocks[0] if len(blocks) == 1 else jnp.concatenate(blocks, axis=axis)


def feed_forward_back(all_normed_two, all_incoming, params, by):
    up_w, down_w, up_vec = params[2], params[3], params[6]
    up_part, down_part = blocks_of(up_w, (by,)), blocks_of(down_w, (by,), 0)
    upper_act = jnp.dot(all_normed_two, up_part, preferred_element_type=jnp.float32)
    upper_act = upper_act + blocks_of(up_vec[None], (by,))
    hidden_f, gate_back = jax.vjp(smooth_gate, upper_act)
    hidden_g = jnp.einsum("rd,fd->rf", all_incoming, down_part, preferred_element_type=jnp.float32)
    return (hidden_f.astype(jnp.bfloat16), gate_back(hidden_g)[0].astype(jnp.bfloat16))


def own_left(rows):
    mine, theirs = blocks_of(rows, (0, 2)), blocks_of(rows, (1, 3))
    return jnp.stack([mine, partner(theirs, 1)])


def up_blocks(own_first, own_second, received, share):
    columns = own_first.shape[1]
    index, count = lax.axis_index("dp"), lax.axis_size("dp")
    total = jnp.zeros((share, count * columns), jnp.float32)
    for by, part in (
        (0, own_first[:share]),
        (2, own_second[:share]),
        (1, received[:, :columns]),
        (3, received[:, columns:]),
    ):
        total = lax.dynamic_update_slice_in_dim(total, part, (index ^ by) * columns, 1)
    return total


def product(left, line, other):
    total = jnp.einsum("rd,re->de", left[0], line, preferred_element_type=jnp.float32)
    return total + jnp.einsum("rd,re->de", left[1], other, preferred_element_type=jnp.float32)


def summed_shares(vector):
    for by in (1, 2):
        vector = vector + partner(vector, by)
    by, count = 1, lax.axis_size("seq")
    while by < count:
        vector = vector + lax.ppermute(vector, "seq", [(i, i ^ by) for i in range(count)])
        by *= 2
    return vector


def by_owner(array, owners):
    rows, columns = array.shape
    return array.reshape(rows, owners, -1).transpose(1, 0, 2).reshape(owners, -1)


def piece_plan(shapes):
    return [
        (which, part * (rows // (2 * pieces)), rows // (2 * pieces), rows // 2)
        for which, (rows, columns) in enumerate(shapes)
        for pieces in (2 if rows * columns > 512 * 1024 else 1,)
        for part in range(pieces)
    ]


def gather_kernel(plan, count, *refs):
    own, full = refs[:count], refs[count : 2 * count]
    (local_sem, own_send, own_recv, far_send, far_recv) = refs[2 * count : 2 * count + 5]
    (side_send, side_recv, near_send, near_recv, last_send, last_recv) = refs[2 * count + 5 :]
    me, place = lax.axis_index("dp"), lax.axis_index("seq")
    far = lax.rem(me + 2, 4)
    near = me + 1 - 2 * lax.rem(me, 2)
    half = lax.rem(place, 2)
    side = place + 1 - 2 * half
    barrier = pltpu.get_barrier_semaphore()
    for target in ({"dp": far}, {"dp": near}, {"seq": side}):
        pl.semaphore_signal(
            barrier, inc=1, device_id=target, device_id_type=pl.DeviceIdType.MESH
        )
    pl.semaphore_wait(barrier, 3)

    def rows_at(which_half, first, rows, half_rows):
        return pl.ds(pl.multiple_of(which_half * half_rows + first, rows), rows)

    def remote(source, target, send, recv, device):
        return pltpu.make_async_remote_copy(
            src_ref=source,
            dst_ref=target,
            send_sem=send,
            recv_sem=recv,
            device_id=device,
            device_id_type=pl.DeviceIdType.MESH,
        )

    far_copies, side_copies, near_copies, last_copies = [], [], [], []
    for index, (which, first, rows, half_rows) in enumerate(plan):
        span = rows_at(half, first, rows, half_rows)
        copy = remote(
            own[which].at[span],
            full[which].at[me, span],
            far_send.at[index],
            far_recv.at[index],
            {"dp": far},
        )
        copy.start()
        far_copies.append(copy)
    own_copies, local_copies = [], []
    for which in range(count):
        copy = remote(
            own[which], full[which].at[me], own_send.at[which], own_recv.at[which], {"dp": near}
        )
        copy.start()
        own_copies.append(copy)
        copy = pltpu.make_async_copy(own[which], full[which].at[me], local_sem.at[which])
        copy.start()
        local_copies.append(copy)

    def last_step(index):
        which, first, rows, half_rows = plan[index]
        side_copies[index].wait_recv()
        block = full[which].at[far, rows_at(1 - half, first, rows, half_rows)]
        copy = remote(block, block, last_send.at[index], last_recv.at[index], {"dp": near})
        copy.start()
        last_copies.append(copy)

    for index, (which, first, rows, half_rows) in enumerate(plan):
        far_copies[index].wait_recv()
        block = full[which].at[far, rows_at(half, first, rows, half_rows)]
        copy = remote(block, block, side_send.at[index], side_recv.at[index], {"seq": side})
        copy.start()
        side_copies.append(copy)
        copy = remote(block, block, near_send.at[index], near_recv.at[index], {"dp": near})
        copy.start()
        near_copies.append(copy)
        if index > 0:
            last_step(index - 1)
    last_step(len(plan) - 1)
    for copy in near_copies + last_copies + own_copies:
        copy.wait_recv()
    for copy in far_copies + side_copies + near_copies + last_copies + own_copies:
        copy.wait_send()
    for copy in local_copies:
        copy.wait()


def gathered_weights(weights):
    owners, places = lax.axis_size("dp"), lax.axis_size("seq")
    if owners != 4 or places % 2:
        return [lax.all_gather(weight, "dp", axis=0, tiled=True) for weight in weights]
    plan = piece_plan([weight.shape for weight in weights])
    count, pieces = len(weights), len(plan)
    dma = pltpu.SemaphoreType.DMA
    full = pl.pallas_call(
        lambda *refs: gather_kernel(plan, count, *refs),
        out_shape=[jax.ShapeDtypeStruct((owners,) + w.shape, w.dtype) for w in weights],
        in_specs=[pl.BlockSpec(memory_space=pltpu.VMEM)] * count,
        out_specs=[pl.BlockSpec(memory_space=pl.ANY)] * count,
        scratch_shapes=[dma((count,))] * 3 + [dma((pieces,))] * 8,
        compiler_params=pltpu.CompilerParams(collective_id=0, has_side_effects=True),
        name="gather_weights",
    )(*weights)
    return [whole.reshape(-1, whole.shape[2]) for whole in full]


def shards(
    ends_in, segments, qkv_weight, out_weight, up_weight, down_weight, gains, shifts, up_bias
):
    section_index = lax.axis_index("section")
    leading = section_index == 0
    outer, inner = lax.axis_size("dp"), lax.axis_size("seq")
    own_slot = ends_in[0]
    seq_count, tok_count, width = own_slot.shape
    share = width // outer
    packed = jnp.concatenate([gains[0].reshape(-1), shifts[0].reshape(-1), up_bias[0]])
    packed = lax.all_gather(packed, "dp", axis=0, tiled=False).astype(jnp.float32)
    gain_count, shift_count = gains.shape[1], shifts.shape[1]

    def rows_of(first, count):
        part = packed[:, first * share : (first + count) * share]
        return part.reshape(outer, count, share).transpose(1, 0, 2).reshape(count, width)

    params = (
        *gathered_weights((qkv_weight[0], out_weight[0], up_weight[0], down_weight[0])),
        rows_of(0, gain_count),
        rows_of(gain_count, shift_count),
        packed[:, (gain_count + shift_count) * share :].reshape(-1),
    )
    bias = score_bias(segments)

    first_output = forward(own_slot, params, bias)[0]
    received = passed_along(
        first_output.astype(jnp.bfloat16).reshape(own_slot.shape), "section", 1
    )
    entry_rows = jnp.where(leading, own_slot, received)
    last_output, saved = forward(entry_rows, params, bias)
    normed_pair, query, own, halo, mixed, residual, normed_two, upper_act = saved
    normed_left = gathered_rows(normed_pair, 1)
    normed_two_sent, normed_left = lax.optimization_barrier((normed_two, normed_left))
    all_normed_two = gathered_tokens(gathered_rows(normed_two_sent))
    mixed_left = gathered_rows(own_left(mixed), 1)
    early_entry = backward(own_slot, entry_rows, params, saved, bias)[0]
    returned = passed_along(
        early_entry.astype(jnp.bfloat16).reshape(own_slot.shape), "section", -1
    )
    incoming = jnp.where(leading, returned, own_slot)
    incoming, all_normed_two, normed_left, mixed_left = lax.optimization_barrier(
        (incoming, all_normed_two, normed_left, mixed_left)
    )
    incoming_line = gathered_rows(incoming.reshape(-1, width))
    entry_g, residual_round, query_g, own_g, vector_grads, incoming_line = backward(
        incoming, entry_rows, params, saved, bias, incoming_line
    )
    first_line = gathered_rows(jnp.concatenate([residual_round, query_g], axis=1))
    second_line = gathered_rows(own_g)
    all_incoming = gathered_tokens(incoming_line)
    hidden, upper_round = feed_forward_back(all_normed_two, all_incoming, params, 0)
    upper_round, hidden, first_line = lax.optimization_barrier((upper_round, hidden, first_line))
    first_other = partner(first_line, 1)
    chip_columns = blocks_of(all_normed_two, (0, 1))
    down_total = jnp.einsum("rf,rd->fd", hidden, all_incoming, preferred_element_type=jnp.float32)
    up_first = jnp.einsum(
        "rd,rf->df", chip_columns, upper_round, preferred_element_type=jnp.float32
    )
    down_total, first_other = lax.optimization_barrier((down_total, first_other))
    out_g = product(mixed_left, first_line[:, :width], first_other[:, :width])
    query_wg = product(normed_left, first_line[:, width:], first_other[:, width:])
    first_sent = jnp.concatenate([out_g[share:], query_wg[share:]], axis=1).astype(jnp.bfloat16)
    vectors_g = jnp.concatenate([by_owner(part, outer) for part in vector_grads], axis=1)
    first_sent, later_incoming, vectors_g = lax.optimization_barrier(
        (first_sent, all_incoming, vectors_g)
    )
    first_sent = partner(first_sent, 2)
    upper_round = feed_forward_back(all_normed_two, later_incoming, params, 2)[1]
    upper_round, second_line, first_sent = lax.optimization_barrier(
        (upper_round, second_line, first_sent)
    )
    second_other = partner(second_line, 1)
    up_second = jnp.einsum(
        "rd,rf->df", chip_columns, upper_round, preferred_element_type=jnp.float32
    )
    own_wg = product(normed_left, second_line, second_other)
    second_sent = partner(own_wg[share:].astype(jnp.bfloat16), 2)
    up_sent = partner(jnp.concatenate([up_first[share:], up_second[share:]], axis=1), 1)
    out_total = out_g[:share] + first_sent[:, :width].astype(jnp.float32)
    qkv_total = jnp.concatenate(
        [
            query_wg[:share] + first_sent[:, width:].astype(jnp.float32),
            own_wg[:share] + second_sent.astype(jnp.float32),
        ],
        axis=1,
    )
    up_total = up_blocks(up_first, up_second, up_sent, share)
    summed = summed_shares(vectors_g.reshape(-1, 128)).reshape(outer, -1)
    own_vectors = lax.dynamic_index_in_dim(summed, lax.axis_index("dp"), 0, keepdims=False)
    gains_total = own_vectors[: gain_count * share].reshape(gain_count, share)
    shifts_total = own_vectors[gain_count * share : (gain_count + shift_count) * share]
    shifts_total = shifts_total.reshape(shift_count, share)
    up_bias_total = own_vectors[(gain_count + shift_count) * share :]

    ends_out = jnp.where(leading, entry_g, last_output).reshape(own_slot.shape)[None]
    return (
        ends_out,
        qkv_total[None],
        out_total[None],
        up_total[None],
        down_total[None],
        gains_total[None],
        shifts_total[None],
        up_bias_total[None],
    )


def solution(mesh):
    in_specs = (
        P("section", "dp", "seq", None),
        P("dp", "seq"),
        P("section", "dp", None),
        P("section", "dp", None),
        P("section", "dp", None),
        P("section", "dp", None),
        P("section", None, "dp"),
        P("section", None, "dp"),
        P("section", "dp"),
    )
    out_specs = (
        P("section", "dp", "seq", None),
        P("section", "dp", None),
        P("section", "dp", None),
        P("section", "dp", None),
        P("section", "dp", None),
        P("section", None, "dp"),
        P("section", None, "dp"),
        P("section", "dp"),
    )
    return jax.shard_map(shards, mesh=mesh, in_specs=in_specs, out_specs=out_specs, check_vma=False)
```
